32 devices in a mesh: seq: 8 (over z, x), tp: 4 (over y, core).
Axes of the slice: x: 2, y: 2, z: 4, core: 2. Of those that a mesh axis runs over, the one named last changes fastest.
Arguments:
- conv_in: bfloat16 [1024, 16384], P('seq', 'tp'), may hold values from -6 to 6
- conv_weight: float32 [4, 16384], P(None, 'tp'), may hold values from -3 to 3
- conv_bias: float32 [16384], P('tp'), may hold values from -0.5 to 0.5
- proj_weight: bfloat16 [16384, 544], P('tp'), may hold values from -0.046875 to 0.046875
- dt_weight: bfloat16 [512, 16384], P(None, 'tp'), may hold values from -0.25 to 0.25
- dt_bias: float32 [16384], P('tp'), may hold values from -6 to -2.5
- decay_rate: float32 [16, 16384], P(None, 'tp'), may hold values from 0.0009765625 to 4
- skip_gain: float32 [16384], P('tp'), may hold values from 0.5 to 1.5
- grad_out: bfloat16 [1024, 16384], P('seq', 'tp'), may hold values from -6 to 6
Outputs:
- mixed: bfloat16 [1024, 16384], P('seq', 'tp')
- weight_grad: float32 [4, 4096, 16], P('tp', 'seq')
The draws below stay inside these ranges and needn't reach their ends.
All inputs are finite; a program needn't handle non-finite values.
Results may differ from the reference program's by a relative error of at most 0.006.
Values may be sent and summed in bfloat16 or wider, within the bound.
No kernel may reach another device: no remote copies, remote signals or barrier semaphores. Data moves between devices by JAX's collectives and lax.ppermute only.
A program may use at most 128 MiB of HBM per device.

```python
import math
import jax
import jax.numpy as jnp
from jax import lax

DI = 16384
NS = 16
RANK = 512
KCONV = 4
TOKENS = 1024
N_TP = 4


def level_of(stream_key, extent, cuts, low, high):
    gain = 1.0
    for axis_at, blocks in cuts:
        heights = jax.random.uniform(jax.random.fold_in(jax.random.fold_in(stream_key, 6), axis_at), (blocks,), jnp.float32, low / len(cuts), high / len(cuts))
        gain = gain * jnp.repeat(jnp.exp(heights), extent[axis_at] // blocks).reshape((-1,) + (1,) * (len(extent) - 1 - axis_at))
    return gain


def centred(own_key, dims, width, most, shards=(), kind=jnp.bfloat16):
    entries = width * jax.random.normal(own_key, dims, jnp.float32)
    if shards:
        entries = entries * level_of(own_key, dims, shards, -0.22, 0.18)
    return jnp.clip(entries, -most, most).astype(kind)


def setup_inputs(seed: int = 0) -> dict:
    streams_of = jax.random.split(jax.random.key(seed), 10)
    conv_in = centred(streams_of[0], (TOKENS, DI), 1.0, 6.0, ((0, 8), (1, 4)))
    conv_weight = centred(streams_of[1], (KCONV, DI), KCONV ** -0.5, 3.0, ((1, 4),), jnp.float32)
    conv_bias = jnp.clip(jax.random.uniform(streams_of[2], (DI,), jnp.float32, -0.5, 0.5) * level_of(streams_of[2], (DI,), ((0, 4),), -0.4, 0.0), -0.5, 0.5)
    proj_weight = centred(streams_of[3], (DI, RANK + 2 * NS), DI ** -0.5, 0.046875, ((0, 4),))
    dt_weight = centred(streams_of[4], (RANK, DI), RANK ** -0.5, 0.25, ((1, 4),))
    dt_bias = jnp.clip(-6.0 + 3.5 * jax.random.uniform(streams_of[5], (DI,), jnp.float32) ** level_of(streams_of[5], (DI,), ((0, 4),), -0.2, 0.2), -6.0, -2.5)
    decay_rate = jnp.clip(jnp.exp(math.log(4.0) - 8.317766 * jax.random.uniform(streams_of[6], (NS, DI), jnp.float32) ** level_of(streams_of[6], (NS, DI), ((1, 4),), -0.2, 0.2)), 0.0009765625, 4.0)
    skip_gain = jnp.clip(0.5 + 1.0 * jax.random.uniform(streams_of[7], (DI,), jnp.float32) ** level_of(streams_of[7], (DI,), ((0, 4),), -0.2, 0.2), 0.5, 1.5)
    grad_out = centred(streams_of[8], (TOKENS, DI), 1.0, 6.0, ((0, 8), (1, 4)))
    return dict(conv_in=conv_in, conv_weight=conv_weight, conv_bias=conv_bias, proj_weight=proj_weight, dt_weight=dt_weight, dt_bias=dt_bias, decay_rate=decay_rate, skip_gain=skip_gain, grad_out=grad_out)


block_len = 16


def reference(conv_in, conv_weight, conv_bias, proj_weight, dt_weight, dt_bias, decay_rate, skip_gain, grad_out):
    inputs = conv_in.astype(jnp.float32)
    padded = jnp.concatenate([jnp.zeros((KCONV - 1, DI), jnp.float32), inputs], axis=0)
    pre_act = conv_bias[None, :] + jnp.zeros((TOKENS, DI), jnp.float32)
    for tap_index in range(KCONV):
        pre_act = pre_act + conv_weight[tap_index][None, :] * padded[tap_index:tap_index + TOKENS]
    conv_out = jax.nn.silu(pre_act).astype(jnp.bfloat16)
    proj_out = jnp.dot(conv_out, proj_weight, preferred_element_type=jnp.float32).astype(jnp.bfloat16)
    dt_low = proj_out[:, :RANK]
    b_matrix = proj_out[:, RANK:RANK + NS].astype(jnp.float32)
    c_matrix = proj_out[:, RANK + NS:].astype(jnp.float32)
    step_size = jax.nn.softplus(jnp.dot(dt_low, dt_weight, preferred_element_type=jnp.float32) + dt_bias[None, :])
    drive_in = step_size * conv_out.astype(jnp.float32)
    scaled_grad = grad_out.astype(jnp.float32) / TOKENS
    blocks = TOKENS // block_len
    slices = (step_size.reshape(blocks, block_len, DI), drive_in.reshape(blocks, block_len, DI),
              b_matrix.reshape(blocks, block_len, NS), c_matrix.reshape(blocks, block_len, NS),
              scaled_grad.reshape(blocks, block_len, DI))

    def block_step(carried, pieces):
        step_now, drive_now, b_now, c_now, grad_now = pieces
        outputs = []
        grads = []
        for offset in range(block_len):
            carried = jnp.exp(-step_now[offset][None, :] * decay_rate) * carried + drive_now[offset][None, :] * b_now[offset][:, None]
            outputs.append(jnp.sum(carried * c_now[offset][:, None], axis=0))
            grads.append(jnp.sum(carried * grad_now[offset][None, :], axis=1))
        return carried, (jnp.stack(outputs), jnp.stack(grads))

    _, (scan_out, grad_parts) = lax.scan(block_step, jnp.zeros((NS, DI), jnp.float32), slices)
    mixed = (scan_out.reshape(TOKENS, DI) + skip_gain[None, :] * conv_out.astype(jnp.float32)).astype(jnp.bfloat16)
    grad_c = grad_parts.reshape(TOKENS, NS).astype(jnp.bfloat16)
    weight_grad = lax.dot_general(conv_out, grad_c, (((0,), (0,)), ((), ())), preferred_element_type=jnp.float32)
    return mixed, weight_grad.reshape(N_TP, DI // N_TP, NS)
```

```python
import math

import jax
import jax.numpy as jnp
from jax import lax
from jax.experimental import pallas as pl
from jax.experimental.pallas import tpu as pltpu
from jax.sharding import PartitionSpec as P

LOG2E = math.log2(math.e)
BLOCK = 16
WIDTH = 512
BF = jnp.bfloat16
F4 = jnp.float32
NT = (((1,), (1,)), ((), ()))
TN = (((0,), (0,)), ((), ()))


def swap(a, axis, bit):
    count = lax.axis_size(axis)
    return lax.ppermute(a, axis, [(i, i ^ bit) for i in range(count)])


def params(limit=48 << 20):
    return pltpu.CompilerParams(
        dimension_semantics=("arbitrary",), vmem_limit_bytes=limit
    )


def conv_kernel(x_ref, rim_ref, w_ref, bias_ref, proj_ref, out_ref, part_ref, ext):
    rows = x_ref.shape[0]
    taps = w_ref.shape[0]
    base = 8 - (taps - 1)

    @pl.when(pl.program_id(0) == 0)
    def _():
        part_ref[...] = jnp.zeros_like(part_ref)

    ext[base:8, :] = rim_ref[...].astype(F4)
    ext[8 : 8 + rows, :] = x_ref[...].astype(F4)
    for top in range(0, rows, BLOCK):
        acc = bias_ref[...] + w_ref[0:1, :] * ext[base + top : base + top + BLOCK, :]
        for tap in range(1, taps):
            at = base + top + tap
            acc = acc + w_ref[tap : tap + 1, :] * ext[at : at + BLOCK, :]
        half = 0.5 * acc
        out_ref[top : top + BLOCK, :] = (half + half * jnp.tanh(half)).astype(BF)
    part_ref[...] += jnp.dot(out_ref[...], proj_ref[...], preferred_element_type=F4)


def conv_project(conv_in, rim, conv_weight, conv_bias, proj_weight):
    rows, channels = conv_in.shape
    taps = conv_weight.shape[0]
    wide = proj_weight.shape[1]
    cols = lambda n: pl.BlockSpec((n, WIDTH), lambda i: (0, i))
    return pl.pallas_call(
        conv_kernel,
        grid=(channels // WIDTH,),
        in_specs=[
            cols(rows),
            cols(taps - 1),
            cols(taps),
            cols(1),
            pl.BlockSpec((WIDTH, wide), lambda i: (i, 0)),
        ],
        out_specs=[cols(rows), pl.BlockSpec((rows, wide), lambda i: (0, 0))],
        out_shape=[
            jax.ShapeDtypeStruct((rows, channels), BF),
            jax.ShapeDtypeStruct((rows, wide), F4),
        ],
        scratch_shapes=[pltpu.VMEM((rows + 8, WIDTH), F4)],
        compiler_params=params(),
        name="conv_project",
    )(conv_in, rim, conv_weight, conv_bias[None], proj_weight)


def spread(rows, states):
    wide = BLOCK * states
    lane = lax.broadcasted_iota(jnp.int32, (states, wide), 1)
    pick = (lane % states == lax.broadcasted_iota(jnp.int32, (states, wide), 0)).astype(BF)
    tiled = jnp.dot(rows, pick, preferred_element_type=F4)
    lane = lax.broadcasted_iota(jnp.int32, (BLOCK, wide), 1)
    own = lane // states == lax.broadcasted_iota(jnp.int32, (BLOCK, wide), 0)
    return jnp.where(own, tiled, 0.0).astype(BF)


def softplus(x):
    u = jnp.exp(-jnp.abs(x))
    small = u * (1.0 - u * (0.5 - u * (1.0 / 3.0)))
    return jnp.maximum(x, 0.0) + jnp.where(u < 0.0078125, small, jnp.log(1.0 + u))


def scan_kernel(
    proj_ref, b_ref, c_ref, dtw_ref, dtb_ref, decay_ref, skip_ref, conv_ref, grad_ref,
    mixed_ref, cum_ref, end_ref, total_ref, pairs_ref,
    step, drive, b_wide, c_wide, hist,
):
    rows = conv_ref.shape[0]
    states = decay_ref.shape[0]
    first = pl.program_id(0) == 0

    @pl.when(first)
    def _():
        pairs_ref[...] = jnp.zeros_like(pairs_ref)
        for top in range(0, rows, BLOCK):
            at = slice(top, top + BLOCK)
            c_wide[at, :] = spread(c_ref[at, :], states)
            b_diag = spread(b_ref[at, :], states)
            ones = jnp.ones((BLOCK, 128), BF)
            b_wide[top * states : (top + BLOCK) * states, :] = lax.dot_general(
                b_diag, ones, TN, preferred_element_type=F4
            )

    tri = (
        lax.broadcasted_iota(jnp.int32, (rows, rows), 0)
        >= lax.broadcasted_iota(jnp.int32, (rows, rows), 1)
    ).astype(BF)
    raw = jnp.dot(proj_ref[...], dtw_ref[...], preferred_element_type=F4)
    step[...] = raw + dtb_ref[...]
    for top in range(0, rows, BLOCK):
        at = slice(top, top + BLOCK)
        now = softplus(step[at, :])
        step[at, :] = now
        conv = conv_ref[at, :].astype(F4)
        drive[at, :] = now * conv
        mixed_ref[at, :] = skip_ref[...] * conv
    high = step[...].astype(BF)
    low = (step[...] - high.astype(F4)).astype(BF)
    cum = jnp.dot(tri, high, preferred_element_type=F4)
    cum_ref[...] = cum + jnp.dot(tri, low, preferred_element_type=F4)
    total_ref[...] = cum_ref[rows - 1 : rows, :]

    rate = decay_ref[...] * (-LOG2E)
    state = jnp.zeros((states, WIDTH), F4)
    for top in range(0, rows, BLOCK):
        slot = (top // BLOCK) % 2
        for t in range(BLOCK):
            r = top + t
            decay = jnp.exp2(step[r : r + 1, :] * rate)
            b_now = b_wide[r * states : (r + 1) * states, :]
            b_now = jnp.concatenate([b_now] * (WIDTH // 128), axis=1)
            state = decay * state + drive[r : r + 1, :] * b_now
            hist[slot, t * states : (t + 1) * states, :] = state.astype(BF)
        at = slice(top, top + BLOCK)
        block = hist[slot]
        mixed_ref[at, :] += jnp.dot(c_wide[at, :], block, preferred_element_type=F4)
        pairs_ref[at, :] += lax.dot_general(
            grad_ref[at, :], block, NT, preferred_element_type=F4
        )
    end_ref[...] = state


def local_scan(proj, b_mat, c_mat, dt_weight, dt_bias, decay_rate, skip, conv_out, grad_out):
    rows, channels = conv_out.shape
    rank = dt_weight.shape[0]
    states = decay_rate.shape[0]
    cols = lambda n: pl.BlockSpec((n, WIDTH), lambda i: (0, i))
    whole = lambda a, b: pl.BlockSpec((a, b), lambda i: (0, 0))
    return pl.pallas_call(
        scan_kernel,
        grid=(channels // WIDTH,),
        in_specs=[
            whole(rows, rank),
            whole(rows, states),
            whole(rows, states),
            cols(rank),
            cols(1),
            cols(states),
            cols(1),
            cols(rows),
            cols(rows),
        ],
        out_specs=[
            cols(rows),
            cols(rows),
            cols(states),
            cols(1),
            whole(rows, BLOCK * states),
        ],
        out_shape=[
            jax.ShapeDtypeStruct((rows, channels), F4),
            jax.ShapeDtypeStruct((rows, channels), F4),
            jax.ShapeDtypeStruct((states, channels), F4),
            jax.ShapeDtypeStruct((1, channels), F4),
            jax.ShapeDtypeStruct((rows, BLOCK * states), F4),
        ],
        scratch_shapes=[
            pltpu.VMEM((rows, WIDTH), F4),
            pltpu.VMEM((rows, WIDTH), F4),
            pltpu.VMEM((rows * states, 128), F4),
            pltpu.VMEM((rows, BLOCK * states), BF),
            pltpu.VMEM((2, BLOCK * states, WIDTH), BF),
        ],
        compiler_params=params(),
        name="local_scan",
    )(proj, b_mat, c_mat, dt_weight, dt_bias[None], decay_rate, skip[None], conv_out, grad_out)


def carry_kernel(
    scale, c_ref, decay_ref, state_ref, cum_ref, mixed_ref, grad_ref, pairs_in,
    out_ref, gradc_ref,
    c_wide, pairs, hist,
):
    rows = cum_ref.shape[0]
    states = decay_ref.shape[0]

    @pl.when(pl.program_id(0) == 0)
    def _():
        pairs[...] = pairs_in[...]
        for top in range(0, rows, BLOCK):
            at = slice(top, top + BLOCK)
            c_wide[at, :] = spread(c_ref[at, :], states)

    rate = decay_ref[...] * (-LOG2E)
    state = state_ref[...]
    for top in range(0, rows, BLOCK):
        slot = (top // BLOCK) % 2
        for t in range(BLOCK):
            r = top + t
            now = jnp.exp2(cum_ref[r : r + 1, :] * rate) * state
            hist[slot, t * states : (t + 1) * states, :] = now.astype(BF)
        at = slice(top, top + BLOCK)
        block = hist[slot]
        more = jnp.dot(c_wide[at, :], block, preferred_element_type=F4)
        out_ref[at, :] = (mixed_ref[at, :] + more).astype(BF)
        pairs[at, :] += lax.dot_general(
            grad_ref[at, :], block, NT, preferred_element_type=F4
        )

    @pl.when(pl.program_id(0) == pl.num_programs(0) - 1)
    def _():
        wide = BLOCK * states
        shape = (rows, wide)
        lane = lax.broadcasted_iota(jnp.int32, shape, 1)
        row = lax.broadcasted_iota(jnp.int32, shape, 0)
        kept = jnp.where(lane // states == row % BLOCK, pairs[...], 0.0) * scale
        pick = (
            lax.broadcasted_iota(jnp.int32, (states, wide), 1) % states
            == lax.broadcasted_iota(jnp.int32, (states, wide), 0)
        ).astype(F4)
        gradc_ref[...] = lax.dot_general(
            pick, kept, NT, preferred_element_type=F4, precision=lax.Precision.HIGHEST
        )


def add_carry(scale, c_mat, decay_rate, incoming, cum, mixed, grad_out, pairs):
    rows, channels = cum.shape
    states = decay_rate.shape[0]
    cols = lambda n: pl.BlockSpec((n, WIDTH), lambda i: (0, i))
    whole = lambda a, b: pl.BlockSpec((a, b), lambda i: (0, 0))

    def body(*refs):
        carry_kernel(scale, *refs)

    return pl.pallas_call(
        body,
        grid=(channels // WIDTH,),
        in_specs=[
            whole(rows, states),
            cols(states),
            cols(states),
            cols(rows),
            cols(rows),
            cols(rows),
            whole(rows, BLOCK * states),
        ],
        out_specs=[cols(rows), whole(states, rows)],
        out_shape=[
            jax.ShapeDtypeStruct((rows, channels), BF),
            jax.ShapeDtypeStruct((states, rows), F4),
        ],
        scratch_shapes=[
            pltpu.VMEM((rows, BLOCK * states), BF),
            pltpu.VMEM((rows, BLOCK * states), F4),
            pltpu.VMEM((2, BLOCK * states, WIDTH), BF),
        ],
        compiler_params=params(),
        name="add_carry",
    )(c_mat, decay_rate, incoming, cum, mixed, grad_out, pairs)


def incoming_state(end, total, decay_rate):
    count = lax.axis_size("seq")
    place = lax.axis_index("seq")
    prefix = jnp.zeros_like(end)
    prefix_sum = jnp.zeros_like(total)
    fade = lambda s: jnp.exp(-decay_rate * s)
    bit = 1
    while bit < count:
        other = swap(end.astype(BF), "seq", bit).astype(F4)
        other_sum = swap(total, "seq", bit)
        later = (place & bit) != 0
        prefix = jnp.where(later, prefix + fade(prefix_sum) * other, prefix)
        prefix_sum = jnp.where(later, prefix_sum + other_sum, prefix_sum)
        end = jnp.where(later, end + fade(total) * other, other + fade(other_sum) * end)
        total = total + other_sum
        bit *= 2
    return prefix


def on_device(
    conv_in,
    conv_weight,
    conv_bias,
    proj_weight,
    dt_weight,
    dt_bias,
    decay_rate,
    skip_gain,
    grad_out,
):
    rows, channels = conv_in.shape
    taps = conv_weight.shape[0]
    rank = dt_weight.shape[0]
    states = decay_rate.shape[0]
    count = lax.axis_size("seq")
    tp = lax.axis_size("tp")
    rim = lax.ppermute(
        conv_in[rows - (taps - 1) :], "seq", [(i, i + 1) for i in range(count - 1)]
    )
    conv_out, part = conv_project(conv_in, rim, conv_weight, conv_bias, proj_weight)
    bit = 1
    while bit < tp:
        mine = part if bit == 1 else part.astype(BF)
        part = mine.astype(F4) + swap(mine, "tp", bit).astype(F4)
        bit *= 2
    proj = part.astype(BF)
    dt_low = proj[:, :rank]
    b_mat = proj[:, rank : rank + states]
    c_mat = proj[:, rank + states :]
    mixed, cum, end, total, pairs = local_scan(
        dt_low, b_mat, c_mat, dt_weight, dt_bias, decay_rate, skip_gain, conv_out, grad_out
    )
    incoming = incoming_state(end, total, decay_rate)
    scale = 1.0 / (rows * count)
    mixed, grad_c = add_carry(
        scale, c_mat, decay_rate, incoming, cum, mixed, grad_out, pairs
    )
    parts = [grad_c] + [swap(grad_c, "tp", k) for k in range(1, tp)]
    grad_c = sum(parts[1:], parts[0]).astype(BF)
    weight = jnp.dot(grad_c, conv_out, preferred_element_type=F4).astype(BF)
    share = channels // count
    weight = weight.reshape(states, count, share).transpose(1, 0, 2)
    weight = lax.all_to_all(weight, "seq", 0, 0)
    weight_grad = jnp.sum(weight.astype(F4), axis=0).T
    return (mixed, weight_grad[None])


def solution(mesh):
    return jax.shard_map(
        on_device,
        mesh=mesh,
        in_specs=(
            P("seq", "tp"),
            P(None, "tp"),
            P("tp"),
            P("tp", None),
            P(None, "tp"),
            P("tp"),
            P(None, "tp"),
            P("tp"),
            P("seq", "tp"),
        ),
        out_specs=(P("seq", "tp"), P("tp", "seq", None)),
        check_vma=False,
    )
```

```python
import math

import jax
import jax.numpy as jnp
from jax import lax
from jax.experimental import pallas as pl
from jax.experimental.pallas import tpu as pltpu
from jax.sharding import PartitionSpec as P

LOG2E = math.log2(math.e)
BLOCK = 16
WIDTH = 512
BF = jnp.bfloat16
F4 = jnp.float32
NT = (((1,), (1,)), ((), ()))
TN = (((0,), (0,)), ((), ()))


def swap(a, axis, bit):
    count = lax.axis_size(axis)
    return lax.ppermute(a, axis, [(i, i ^ bit) for i in range(count)])


def params(limit=12 << 20):
    return pltpu.CompilerParams(vmem_limit_bytes=limit)


def cols(rows):
    return pl.BlockSpec((rows, WIDTH), lambda i: (0, i))


def whole(rows, lanes):
    return pl.BlockSpec((rows, lanes), lambda i: (0, 0))


def fetch(*arrays):
    count = len(arrays)

    def body(*refs):
        sems = refs[-1]
        copies = [
            pltpu.make_async_copy(refs[i], refs[count + i], sems.at[i]) for i in range(count)
        ]
        for copy in copies:
            copy.start()
        for copy in copies:
            copy.wait()

    moved = 2 * sum(a.size * a.dtype.itemsize for a in arrays)
    return pl.pallas_call(
        body,
        in_specs=[pl.BlockSpec(memory_space=pltpu.HBM)] * count,
        out_specs=in_vmem(count),
        out_shape=[pltpu.VMEM(a.shape, a.dtype) for a in arrays],
        scratch_shapes=[pltpu.SemaphoreType.DMA((count,))],
        compiler_params=params(1 << 20),
        cost_estimate=pl.CostEstimate(flops=0, bytes_accessed=moved, transcendentals=0),
        name="fetch",
    )(*[in_hbm(a) for a in arrays])


def chunk_at(i, base=0):
    return pl.ds(pl.multiple_of((base + i) * WIDTH, WIDTH), WIDTH)


def conv_kernel(x_ref, odd_ref, even_ref, w_ref, bias_ref, proj_ref, out_ref, part_ref, ext):
    rows, channels = x_ref.shape
    rim = odd_ref.shape[0]
    taps = w_ref.shape[0]
    base = rim - (taps - 1)
    odd = (lax.axis_index("seq") & 1) != 0
    part_ref[...] = jnp.zeros_like(part_ref)

    @pl.loop(0, channels // WIDTH)
    def _(i):
        for j in range(WIDTH // 128):
            lanes = pl.ds(pl.multiple_of(i * WIDTH + j * 128, 128), 128)
            ext[j, 0:rim, :] = jnp.where(
                odd, odd_ref[:, lanes].astype(F4), even_ref[:, lanes].astype(F4)
            )
            ext[j, rim : rim + rows, :] = x_ref[:, lanes].astype(F4)
            weights = w_ref[:, lanes]
            bias = bias_ref[:, lanes]
            for top in range(0, rows, BLOCK):
                acc = bias
                for tap in range(taps):
                    at = base + top + tap
                    acc = acc + weights[tap : tap + 1, :] * ext[j, at : at + BLOCK, :]
                half = 0.5 * acc
                out_ref[top : top + BLOCK, lanes] = (half + half * jnp.tanh(half)).astype(BF)
        at = chunk_at(i)
        part_ref[...] += lax.dot_general(
            out_ref[:, at], proj_ref[:, at], NT, preferred_element_type=F4
        )


def conv_project(conv_in, rims, conv_weight, conv_bias, proj_weight_t):
    rows, channels = conv_in.shape
    wide = proj_weight_t.shape[0]
    rim = rims[0].shape[0]
    return pl.pallas_call(
        conv_kernel,
        in_specs=in_vmem(6),
        out_specs=in_vmem(2),
        out_shape=[
            jax.ShapeDtypeStruct((rows, channels), BF),
            jax.ShapeDtypeStruct((rows, wide), F4),
        ],
        scratch_shapes=[pltpu.VMEM((WIDTH // 128, rows + rim, 128), F4)],
        compiler_params=params(),
        name="conv_project",
    )(conv_in, *rims, conv_weight, conv_bias, proj_weight_t)


def in_hbm(a):
    return pltpu.with_memory_space_constraint(a, pltpu.HBM)


def in_vmem(count):
    return [pl.BlockSpec(memory_space=pltpu.VMEM)] * count


def split_sum(total, rank, out_ref):
    wide = total.shape[1]
    high = total.astype(BF)
    out_ref[:, :wide] = high
    out_ref[:, wide:] = (total[:, rank:] - high[:, rank:].astype(F4)).astype(BF)


def joined(ref, wide, rank):
    high = ref[:, :wide].astype(F4)
    return high[:, :rank], high[:, rank:] + ref[:, wide:].astype(F4)


def add_first(part, other, rank):
    rows, wide = part.shape

    def body(a_ref, b_ref, out_ref):
        split_sum(a_ref[...] + b_ref[...], rank, out_ref)

    return pl.pallas_call(
        body,
        in_specs=in_vmem(2),
        out_specs=pl.BlockSpec(memory_space=pltpu.VMEM),
        out_shape=jax.ShapeDtypeStruct((rows, 2 * wide - rank), BF),
        compiler_params=params(),
        name="add_first",
    )(part, other)


def add_later(mine, other, wide, rank):
    def body(a_ref, b_ref, out_ref):
        a_low, a_high = joined(a_ref, wide, rank)
        b_low, b_high = joined(b_ref, wide, rank)
        total = jnp.concatenate([a_low + b_low, a_high + b_high], axis=1)
        split_sum(total, rank, out_ref)

    return pl.pallas_call(
        body,
        in_specs=in_vmem(2),
        out_specs=pl.BlockSpec(memory_space=pltpu.VMEM),
        out_shape=jax.ShapeDtypeStruct(mine.shape, BF),
        compiler_params=params(),
        name="add_later",
    )(mine, other)


def softplus(x):
    u = jnp.exp(-jnp.abs(x))
    small = u * (1.0 - u * (0.5 - u * (1.0 / 3.0)))
    return jnp.maximum(x, 0.0) + jnp.where(u < 0.0078125, small, jnp.log(1.0 + u))


def wide_iota(shape, axis):
    return lax.broadcasted_iota(jnp.int32, shape, axis)


def contract(block, c_now, grad_now):
    mixed = jnp.dot(c_now, block, preferred_element_type=F4)
    pairs = lax.dot_general(grad_now, block, NT, preferred_element_type=F4)
    return mixed, pairs


def prepare_kernel(mine_ref, other_ref, proj_ref, b_ref, c_ref, alt_ref):
    rows, rank = proj_ref.shape
    wide = c_ref.shape[1]
    states = wide // BLOCK
    a_low, a_high = joined(mine_ref, rank + 2 * states, rank)
    b_low, b_high = joined(other_ref, rank + 2 * states, rank)
    proj_ref[...] = (a_low + b_low).astype(BF)
    ends = (a_high + b_high).astype(BF)
    lane = wide_iota((states, wide), 1)
    row = wide_iota((states, wide), 0)
    by_token = (lane % states == row).astype(BF)
    by_state = (lane // BLOCK == row).astype(BF)
    lane = wide_iota((rows, wide), 1)
    row = wide_iota((rows, wide), 0) % BLOCK
    c_mat = ends[:, states:]
    tiled = jnp.dot(c_mat, by_token, preferred_element_type=F4)
    c_ref[...] = jnp.where(lane // states == row, tiled, 0.0).astype(BF)
    tiled = jnp.dot(c_mat, by_state, preferred_element_type=F4)
    alt_ref[...] = jnp.where(lane % BLOCK == row, tiled, 0.0).astype(BF)
    tiled = jnp.dot(ends[:, :states], by_token, preferred_element_type=F4)
    b_diag = jnp.where(lane // states == row, tiled, 0.0).astype(BF)
    ones = jnp.ones((BLOCK, 128), BF)
    for top in range(0, rows, BLOCK):
        b_ref[top * states : (top + BLOCK) * states, :] = lax.dot_general(
            b_diag[top : top + BLOCK, :], ones, TN, preferred_element_type=F4
        )


def prepare(mine, other, rank, states):
    rows = mine.shape[0]
    wide = BLOCK * states
    return pl.pallas_call(
        prepare_kernel,
        in_specs=in_vmem(2),
        out_specs=in_vmem(4),
        out_shape=[
            jax.ShapeDtypeStruct((rows, rank), BF),
            jax.ShapeDtypeStruct((rows * states, 128), F4),
            jax.ShapeDtypeStruct((rows, wide), BF),
            jax.ShapeDtypeStruct((rows, wide), BF),
        ],
        compiler_params=params(),
        name="prepare",
    )(mine, other)


def scan_kernel(
    base, fresh,
    proj_ref, b_ref, c_ref, dtw_ref, dtb_ref, rate_ref, skip_ref, conv_ref, grad_ref, pairs_in,
    mixed_ref, cum_ref, end_ref, send_ref, total_ref, pairs_ref,
    raw, step, drive, even, odd,
):
    rows = conv_ref.shape[0]
    states = rate_ref.shape[0]
    chunks = mixed_ref.shape[1] // WIDTH
    pairs_ref[...] = jnp.zeros_like(pairs_ref) if fresh else pairs_in[...]
    tri = (
        wide_iota((rows, 2 * rows), 0) >= wide_iota((rows, 2 * rows), 1) % rows
    ).astype(BF)

    def project(i):
        raw[...] = jnp.dot(proj_ref[...], dtw_ref[:, chunk_at(i, base)], preferred_element_type=F4)

    project(0)

    @pl.loop(0, chunks)
    def _(i):
        here = chunk_at(i)
        at_in = chunk_at(i, base)
        bias = dtb_ref[:, at_in]
        skip = skip_ref[:, at_in]
        highs = []
        lows = []
        for top in range(0, rows, BLOCK):
            at = slice(top, top + BLOCK)
            now = softplus(raw[at, :] + bias)
            step[at, :] = now
            conv = conv_ref[at, at_in].astype(F4)
            drive[at, :] = now * conv
            mixed_ref[at, here] = skip * conv
            high = now.astype(BF)
            highs.append(high)
            lows.append((now - high.astype(F4)).astype(BF))
        cum_ref[:, here] = jnp.dot(
            tri, jnp.concatenate(highs + lows, axis=0), preferred_element_type=F4
        )
        total_ref[:, here] = cum_ref[rows - 1 : rows, here]
        project(jnp.minimum(i + 1, chunks - 1))

        rate = rate_ref[:, at_in]
        state = jnp.zeros((states, WIDTH), F4)
        for top in range(0, rows, BLOCK):
            hist = odd if (top // BLOCK) % 2 else even
            for t in range(BLOCK):
                r = top + t
                b_now = b_ref[r * states : (r + 1) * states, :]
                b_now = jnp.concatenate([b_now] * (WIDTH // 128), axis=1)
                state = (
                    jnp.exp2(step[r : r + 1, :] * rate) * state + drive[r : r + 1, :] * b_now
                )
                hist[t * states : (t + 1) * states, :] = state.astype(BF)
            at = slice(top, top + BLOCK)
            mixed, pairs = contract(hist[...], c_ref[at, :], grad_ref[at, at_in])
            mixed_ref[at, here] += mixed
            pairs_ref[at, :] += pairs
        end_ref[:, here] = state
        send_ref[:, here] = state.astype(BF)


def local_scan(base, width, prepared, dt_weight, dt_bias, rate, skip, conv_out, grad_out, pairs):
    rows = conv_out.shape[0]
    states = rate.shape[0]
    wide = BLOCK * states
    fresh = pairs is None
    proj, b_wide, c_wide, _ = prepared

    def body(*refs):
        refs = list(refs)
        if fresh:
            refs.insert(9, None)
        scan_kernel(base, fresh, *refs)

    ops = [proj, b_wide, c_wide, dt_weight, dt_bias, rate, skip, conv_out, grad_out]
    ops += [] if fresh else [pairs]
    work = rows * width * states
    return pl.pallas_call(
        body,
        in_specs=in_vmem(len(ops)),
        out_specs=in_vmem(6),
        out_shape=[
            jax.ShapeDtypeStruct((rows, width), F4),
            jax.ShapeDtypeStruct((rows, width), F4),
            jax.ShapeDtypeStruct((states, width), F4),
            jax.ShapeDtypeStruct((states, width), BF),
            jax.ShapeDtypeStruct((1, width), F4),
            jax.ShapeDtypeStruct((rows, wide), F4),
        ],
        scratch_shapes=[
            pltpu.VMEM((rows, WIDTH), F4),
            pltpu.VMEM((rows, WIDTH), F4),
            pltpu.VMEM((rows, WIDTH), F4),
            pltpu.VMEM((wide, WIDTH), BF),
            pltpu.VMEM((wide, WIDTH), BF),
        ],
        compiler_params=params(),
        cost_estimate=pl.CostEstimate(
            flops=600 * work, bytes_accessed=work, transcendentals=work
        ),
        name="local_scan",
    )(*ops)


def carry_kernel(
    base, scale, fresh, final,
    alt_ref, rate_ref, state_ref, cum_ref, mixed_ref, grad_ref, pairs_in, local_ref, prev_ref,
    out_ref, result_ref,
    pairs, rates, inits, even, odd,
):
    rows = cum_ref.shape[0]
    states = rate_ref.shape[0]
    wide = BLOCK * states
    i = pl.program_id(0)

    @pl.when(i == 0)
    def _():
        pairs[...] = jnp.zeros_like(pairs) if fresh else pairs_in[...]

    here = chunk_at(i)
    at_in = chunk_at(i, base)
    for n in range(states):
        at = slice(n * BLOCK, (n + 1) * BLOCK)
        shape = (BLOCK, WIDTH)
        rates[at, :] = jnp.broadcast_to(rate_ref[n : n + 1, at_in], shape).astype(BF)
        inits[at, :] = jnp.broadcast_to(state_ref[n : n + 1, here], shape).astype(BF)
    for top in range(0, rows, BLOCK):
        hist = odd if (top // BLOCK) % 2 else even
        tokens = slice(top, top + BLOCK)
        cum = cum_ref[tokens, here].astype(BF)
        for n in range(states):
            at = slice(n * BLOCK, (n + 1) * BLOCK)
            hist[at, :] = jnp.exp2(cum * rates[at, :]) * inits[at, :]
        mixed, more = contract(hist[...], alt_ref[tokens, :], grad_ref[tokens, at_in])
        out_ref[tokens, :] = (mixed_ref[tokens, here] + mixed).astype(BF)
        pairs[tokens, :] += more

    @pl.when(i == pl.num_programs(0) - 1)
    def _():
        if not final:
            result_ref[...] = pairs[...]
            return
        lane = wide_iota((rows, wide), 1)
        row = wide_iota((rows, wide), 0) % BLOCK
        by_state = jnp.where(lane % BLOCK == row, pairs[...], 0.0) * scale
        by_token = jnp.where(lane // states == row, local_ref[...], 0.0) * scale
        lane = wide_iota((states, wide), 1)
        row = wide_iota((states, wide), 0)
        exact = dict(preferred_element_type=F4, precision=lax.Precision.HIGHEST)
        result_ref[...] = lax.dot_general(
            (lane // BLOCK == row).astype(F4), by_state, NT, **exact
        ) + lax.dot_general((lane % states == row).astype(F4), by_token, NT, **exact)


def add_carry(base, scale, alt, rate, incoming, cum, mixed, grad_out, pairs, local, prev):
    rows, width = cum.shape
    states, channels = rate.shape
    wide = BLOCK * states
    fresh, final = pairs is None, local is not None
    ops = [alt, rate, incoming, cum, mixed, grad_out]
    extra = [pairs, local, prev]
    specs = in_vmem(6)
    for a in extra:
        if a is not None:
            ops.append(a)
            specs += [pl.BlockSpec(memory_space=pl.ANY)] if a is prev else in_vmem(1)

    def body(*refs):
        refs = list(refs)
        for k, a in enumerate(extra):
            if a is None:
                refs.insert(6 + k, None)
        carry_kernel(base, scale, fresh, final, *refs)

    work = rows * width * states
    return pl.pallas_call(
        body,
        grid=(width // WIDTH,),
        in_specs=specs,
        out_specs=[
            pl.BlockSpec((rows, WIDTH), lambda i: (0, i + base)),
            whole(states, rows) if final else whole(rows, wide),
        ],
        out_shape=[
            jax.ShapeDtypeStruct((rows, channels), BF),
            jax.ShapeDtypeStruct((states, rows) if final else (rows, wide), F4),
        ],
        scratch_shapes=[
            pltpu.VMEM((rows, wide), F4),
            pltpu.VMEM((wide, WIDTH), BF),
            pltpu.VMEM((wide, WIDTH), BF),
            pltpu.VMEM((wide, WIDTH), BF),
            pltpu.VMEM((wide, WIDTH), BF),
        ],
        input_output_aliases={} if prev is None else {len(ops) - 1: 0},
        compiler_params=params(),
        cost_estimate=pl.CostEstimate(
            flops=300 * work, bytes_accessed=work, transcendentals=work
        ),
        name="add_carry",
    )(*ops)


def merge_kernel(bit, last, rate_ref, end_ref, total_ref, other_ref, osum_ref, pre_ref, psum_ref, *outs):
    later = (lax.axis_index("seq") & bit) != 0
    rate = rate_ref[...]
    fade = lambda s: jnp.exp2(rate * s)
    other = other_ref[...].astype(F4)
    prefix = pre_ref[...]
    outs[0][...] = jnp.where(later, prefix + fade(psum_ref[...]) * other, prefix)
    if not last:
        total, osum, end = total_ref[...], osum_ref[...], end_ref[...]
        outs[1][...] = jnp.where(later, psum_ref[...] + osum, psum_ref[...])
        first = jnp.where(later, other, end)
        second = jnp.where(later, end, other)
        end = second + fade(jnp.where(later, total, osum)) * first
        outs[2][...] = end
        outs[3][...] = end.astype(BF)
        outs[4][...] = total + osum


def merge(base, bit, last, rate, end, total, other, other_sum, prefix, prefix_sum):
    states, channels = end.shape
    many = jax.ShapeDtypeStruct((states, channels), F4)
    one = jax.ShapeDtypeStruct((1, channels), F4)
    outs = [many] if last else [many, one, many, jax.ShapeDtypeStruct((states, channels), BF), one]
    wide, narrow = cols(states), cols(1)

    def body(*refs):
        merge_kernel(bit, last, *refs)

    return pl.pallas_call(
        body,
        grid=(channels // WIDTH,),
        in_specs=[
            pl.BlockSpec((states, WIDTH), lambda i: (0, i + base)),
            wide, narrow, wide, narrow, wide, narrow,
        ],
        out_specs=[wide] if last else [wide, narrow, wide, wide, narrow],
        out_shape=outs,
        compiler_params=params(),
        name="merge",
    )(rate, end, total, other, other_sum, prefix, prefix_sum)


def weight_first(parts, conv_out, count):
    states, rows = parts[0].shape
    share = conv_out.shape[1] // count
    many = len(parts)

    def body(*refs):
        conv_ref, out_ref = refs[many:]
        grad_c = refs[0][...]
        for r in refs[1:many]:
            grad_c = grad_c + r[...]
        grad_c = grad_c.astype(BF)
        for j in range(count):
            block = conv_ref[:, j * share : (j + 1) * share]
            out_ref[j] = jnp.dot(grad_c, block, preferred_element_type=F4).astype(BF)

    return pl.pallas_call(
        body,
        in_specs=in_vmem(many + 1),
        out_specs=pl.BlockSpec(memory_space=pltpu.VMEM),
        out_shape=jax.ShapeDtypeStruct((count, states, share), BF),
        compiler_params=params(),
        name="weight_first",
    )(*parts, conv_out)


def weight_gradient(parts, conv_out):
    count = lax.axis_size("seq")
    states = parts[0].shape[0]
    share = conv_out.shape[1] // count
    if share % 128 == 0:
        weight = weight_first(parts, conv_out, count)
    else:
        grad_c = sum(parts[1:], parts[0]).astype(BF)
        weight = jnp.dot(grad_c, conv_out, preferred_element_type=F4).astype(BF)
        weight = weight.reshape(states, count, share).transpose(1, 0, 2)
    weight = lax.all_to_all(weight, "seq", 0, 0)
    return jnp.sum(weight.astype(F4), axis=0).T


def exchange(base, bit, rate, held):
    end, send, total, prefix, prefix_sum = held
    last = 2 * bit >= lax.axis_size("seq")
    other = swap(send, "seq", bit)
    other_sum = total if last else swap(total, "seq", bit)
    outs = merge(base, bit, last, rate, end, total, other, other_sum, prefix, prefix_sum)
    if last:
        return outs[0]
    prefix, prefix_sum, end, send, total = outs
    return end, send, total, prefix, prefix_sum


def on_device(
    conv_in,
    conv_weight,
    conv_bias,
    proj_weight,
    dt_weight,
    dt_bias,
    decay_rate,
    skip_gain,
    grad_out,
):
    rows, channels = conv_in.shape
    taps = conv_weight.shape[0]
    rank = dt_weight.shape[0]
    states = decay_rate.shape[0]
    count = lax.axis_size("seq")
    tp = lax.axis_size("tp")
    rim_rows = 8 * -(-(taps - 1) // 8)
    edge = conv_in[rows - rim_rows :]
    rims = [
        lax.ppermute(edge, "seq", [p for i in range(k, count - 1, 2) for p in ((i, i + 1), (i + 1, i))])
        for k in range(2)
    ]
    x, w, bias, weight_t = fetch(conv_in, conv_weight, conv_bias[None], proj_weight.T)
    rate = decay_rate * (-LOG2E)
    conv_out, part = conv_project(x, rims, w, bias, weight_t)
    mine = add_first(part, swap(part, "tp", 1), rank)
    other = swap(mine, "tp", 2)
    bit = 4
    while bit < tp:
        mine = add_later(mine, other, part.shape[1], rank)
        other = swap(mine, "tp", bit)
        bit *= 2
    prepared = prepare(mine, other, rank, states)

    width = channels // 2
    bases = (0, width // WIDTH)
    pairs = None
    local, held = [], []
    for base in bases:
        mixed, cum, end, send, total, pairs = local_scan(
            base, width, prepared, dt_weight, dt_bias[None], rate, skip_gain[None],
            conv_out, grad_out, pairs,
        )
        local.append((cum, mixed))
        held.append((end, send, total, jnp.zeros_like(end), jnp.zeros_like(total)))
    bit = 1
    while bit < count:
        held = [exchange(base, bit, rate, h) for base, h in zip(bases, held)]
        bit *= 2

    scale = 1.0 / (rows * count)
    shared = (scale, prepared[3], rate)
    mixed, more = add_carry(bases[0], *shared, held[0], *local[0], grad_out, None, None, None)
    mixed, grad_c = add_carry(bases[1], *shared, held[1], *local[1], grad_out, more, pairs, mixed)
    parts = [grad_c] + [swap(grad_c, "tp", k) for k in range(1, tp)]
    weight_grad = weight_gradient(parts, conv_out)
    return (mixed, weight_grad[None])


def solution(mesh):
    return jax.shard_map(
        on_device,
        mesh=mesh,
        in_specs=(
            P("seq", "tp"),
            P(None, "tp"),
            P("tp"),
            P("tp", None),
            P(None, "tp"),
            P("tp"),
            P(None, "tp"),
            P("tp"),
            P("seq", "tp"),
        ),
        out_specs=(P("seq", "tp"), P("tp", "seq", None)),
        check_vma=False,
    )
```

```python
import math

import jax
import jax.numpy as jnp
from jax import lax
from jax.experimental import pallas as pl
from jax.experimental.pallas import tpu as pltpu
from jax.sharding import PartitionSpec as P

LOG2E = math.log2(math.e)
BLOCK = 16
WIDTH = 512
BF = jnp.bfloat16
F4 = jnp.float32
NT = (((1,), (1,)), ((), ()))
TN = (((0,), (0,)), ((), ()))


def swap(a, axis, bit):
    count = lax.axis_size(axis)
    return lax.ppermute(a, axis, [(i, i ^ bit) for i in range(count)])


def params(limit=12 << 20):
    return pltpu.CompilerParams(vmem_limit_bytes=limit)


def cols(rows):
    return pl.BlockSpec((rows, WIDTH), lambda i: (0, i))


def whole(rows, lanes):
    return pl.BlockSpec((rows, lanes), lambda i: (0, 0))


def fetch(*arrays):
    count = len(arrays)

    def body(*refs):
        sems = refs[-1]
        copies = [
            pltpu.make_async_copy(refs[i], refs[count + i], sems.at[i]) for i in range(count)
        ]
        for copy in copies:
            copy.start()
        for copy in copies:
            copy.wait()

    moved = 2 * sum(a.size * a.dtype.itemsize for a in arrays)
    return pl.pallas_call(
        body,
        in_specs=[pl.BlockSpec(memory_space=pltpu.HBM)] * count,
        out_specs=in_vmem(count),
        out_shape=[pltpu.VMEM(a.shape, a.dtype) for a in arrays],
        scratch_shapes=[pltpu.SemaphoreType.DMA((count,))],
        compiler_params=params(1 << 20),
        cost_estimate=pl.CostEstimate(flops=0, bytes_accessed=moved, transcendentals=0),
        name="fetch",
    )(*[in_hbm(a) for a in arrays])


def chunk_at(i, base=0):
    return pl.ds(pl.multiple_of((base + i) * WIDTH, WIDTH), WIDTH)


def conv_kernel(x_ref, odd_ref, even_ref, w_ref, bias_ref, proj_ref, out_ref, part_ref, ext):
    rows, channels = x_ref.shape
    rim = odd_ref.shape[0]
    taps = w_ref.shape[0]
    base = rim - (taps - 1)
    odd = (lax.axis_index("seq") & 1) != 0
    part_ref[...] = jnp.zeros_like(part_ref)

    @pl.loop(0, channels // WIDTH)
    def _(i):
        for j in range(WIDTH // 128):
            lanes = pl.ds(pl.multiple_of(i * WIDTH + j * 128, 128), 128)
            ext[j, 0:rim, :] = jnp.where(
                odd, odd_ref[:, lanes].astype(F4), even_ref[:, lanes].astype(F4)
            )
            ext[j, rim : rim + rows, :] = x_ref[:, lanes].astype(F4)
            weights = w_ref[:, lanes]
            bias = bias_ref[:, lanes]
            for top in range(0, rows, BLOCK):
                acc = bias
                for tap in range(taps):
                    at = base + top + tap
                    acc = acc + weights[tap : tap + 1, :] * ext[j, at : at + BLOCK, :]
                half = 0.5 * acc
                out_ref[top : top + BLOCK, lanes] = (half + half * jnp.tanh(half)).astype(BF)
        at = chunk_at(i)
        part_ref[...] += lax.dot_general(
            out_ref[:, at], proj_ref[:, at], NT, preferred_element_type=F4
        )


def conv_project(conv_in, rims, conv_weight, conv_bias, proj_weight_t):
    rows, channels = conv_in.shape
    wide = proj_weight_t.shape[0]
    rim = rims[0].shape[0]
    return pl.pallas_call(
        conv_kernel,
        in_specs=in_vmem(6),
        out_specs=in_vmem(2),
        out_shape=[
            jax.ShapeDtypeStruct((rows, channels), BF),
            jax.ShapeDtypeStruct((rows, wide), F4),
        ],
        scratch_shapes=[pltpu.VMEM((WIDTH // 128, rows + rim, 128), F4)],
        compiler_params=params(),
        name="conv_project",
    )(conv_in, *rims, conv_weight, conv_bias, proj_weight_t)


def in_hbm(a):
    return pltpu.with_memory_space_constraint(a, pltpu.HBM)


def in_vmem(count):
    return [pl.BlockSpec(memory_space=pltpu.VMEM)] * count


def split_sum(total, rank, out_ref):
    wide = total.shape[1]
    high = total.astype(BF)
    out_ref[:, :wide] = high
    out_ref[:, wide:] = (total[:, rank:] - high[:, rank:].astype(F4)).astype(BF)


def joined(ref, wide, rank):
    high = ref[:, :wide].astype(F4)
    return high[:, :rank], high[:, rank:] + ref[:, wide:].astype(F4)


def add_first(part, other, rank):
    rows, wide = part.shape

    def body(a_ref, b_ref, out_ref):
        split_sum(a_ref[...] + b_ref[...], rank, out_ref)

    return pl.pallas_call(
        body,
        in_specs=in_vmem(2),
        out_specs=pl.BlockSpec(memory_space=pltpu.VMEM),
        out_shape=jax.ShapeDtypeStruct((rows, 2 * wide - rank), BF),
        compiler_params=params(),
        name="add_first",
    )(part, other)


def add_later(mine, other, wide, rank):
    def body(a_ref, b_ref, out_ref):
        a_low, a_high = joined(a_ref, wide, rank)
        b_low, b_high = joined(b_ref, wide, rank)
        total = jnp.concatenate([a_low + b_low, a_high + b_high], axis=1)
        split_sum(total, rank, out_ref)

    return pl.pallas_call(
        body,
        in_specs=in_vmem(2),
        out_specs=pl.BlockSpec(memory_space=pltpu.VMEM),
        out_shape=jax.ShapeDtypeStruct(mine.shape, BF),
        compiler_params=params(),
        name="add_later",
    )(mine, other)


def softplus(x):
    u = jnp.exp(-jnp.abs(x))
    small = u * (1.0 - u * (0.5 - u * (1.0 / 3.0)))
    return jnp.maximum(x, 0.0) + jnp.where(u < 0.0078125, small, jnp.log(1.0 + u))


def wide_iota(shape, axis):
    return lax.broadcasted_iota(jnp.int32, shape, axis)


def contract(block, c_now, grad_now):
    mixed = jnp.dot(c_now, block, preferred_element_type=F4)
    pairs = lax.dot_general(grad_now, block, NT, preferred_element_type=F4)
    return mixed, pairs


def prepare_kernel(mine_ref, other_ref, proj_ref, b_ref, c_ref, alt_ref):
    rows, rank = proj_ref.shape
    wide = c_ref.shape[1]
    states = wide // BLOCK
    a_low, a_high = joined(mine_ref, rank + 2 * states, rank)
    b_low, b_high = joined(other_ref, rank + 2 * states, rank)
    proj_ref[...] = (a_low + b_low).astype(BF)
    ends = (a_high + b_high).astype(BF)
    lane = wide_iota((states, wide), 1)
    row = wide_iota((states, wide), 0)
    by_token = (lane % states == row).astype(BF)
    by_state = (lane // BLOCK == row).astype(BF)
    lane = wide_iota((rows, wide), 1)
    row = wide_iota((rows, wide), 0) % BLOCK
    c_mat = ends[:, states:]
    tiled = jnp.dot(c_mat, by_token, preferred_element_type=F4)
    c_ref[...] = jnp.where(lane // states == row, tiled, 0.0).astype(BF)
    tiled = jnp.dot(c_mat, by_state, preferred_element_type=F4)
    alt_ref[...] = jnp.where(lane % BLOCK == row, tiled, 0.0).astype(BF)
    tiled = jnp.dot(ends[:, :states], by_token, preferred_element_type=F4)
    b_diag = jnp.where(lane // states == row, tiled, 0.0).astype(BF)
    ones = jnp.ones((BLOCK, 128), BF)
    for top in range(0, rows, BLOCK):
        b_ref[top * states : (top + BLOCK) * states, :] = lax.dot_general(
            b_diag[top : top + BLOCK, :], ones, TN, preferred_element_type=F4
        )


def prepare(mine, other, rank, states):
    rows = mine.shape[0]
    wide = BLOCK * states
    return pl.pallas_call(
        prepare_kernel,
        in_specs=in_vmem(2),
        out_specs=in_vmem(4),
        out_shape=[
            jax.ShapeDtypeStruct((rows, rank), BF),
            jax.ShapeDtypeStruct((rows * states, 128), F4),
            jax.ShapeDtypeStruct((rows, wide), BF),
            jax.ShapeDtypeStruct((rows, wide), BF),
        ],
        compiler_params=params(),
        name="prepare",
    )(mine, other)


def pack_sums(total_ref, send_ref, folded):
    states, per = folded.shape
    width = states * per
    for n in range(states):
        folded[n : n + 1, :] = total_ref[:, n * per : (n + 1) * per]
    high = folded[...].astype(BF)
    send_ref[:, width : width + per] = high
    send_ref[:, width + per :] = (folded[...] - high.astype(F4)).astype(BF)


def unpack_sums(got_ref, sum_ref, folded):
    states, per = folded.shape
    width = states * per
    folded[...] = got_ref[:, width : width + per].astype(F4) + got_ref[:, width + per :].astype(F4)
    for n in range(states):
        sum_ref[:, n * per : (n + 1) * per] = folded[n : n + 1, :]


def message_width(width, states):
    return width + 2 * (width // states)


def scan_kernel(
    base, fresh,
    proj_ref, b_ref, c_ref, dtw_ref, dtb_ref, rate_ref, skip_ref, conv_ref, grad_ref, pairs_in,
    mixed_ref, cum_ref, end_ref, send_ref, total_ref, pairs_ref,
    raw, step, drive, folded, even, odd,
):
    rows = conv_ref.shape[0]
    states = rate_ref.shape[0]
    chunks = mixed_ref.shape[1] // WIDTH
    pairs_ref[...] = jnp.zeros_like(pairs_ref) if fresh else pairs_in[...]
    tri = (wide_iota((rows, rows), 0) >= wide_iota((rows, rows), 1)).astype(BF)

    def project(i):
        raw[...] = jnp.dot(proj_ref[...], dtw_ref[:, chunk_at(i, base)], preferred_element_type=F4)

    project(0)

    @pl.loop(0, chunks)
    def _(i):
        here = chunk_at(i)
        at_in = chunk_at(i, base)
        bias = dtb_ref[:, at_in]
        skip = skip_ref[:, at_in]
        rounded = []
        for top in range(0, rows, BLOCK):
            at = slice(top, top + BLOCK)
            now = softplus(raw[at, :] + bias)
            step[at, :] = now
            conv = conv_ref[at, at_in].astype(F4)
            drive[at, :] = now * conv
            mixed_ref[at, here] = skip * conv
            rounded.append(now.astype(BF))
        cum_ref[:, here] = jnp.dot(
            tri, jnp.concatenate(rounded, axis=0), preferred_element_type=F4
        )
        total_ref[:, here] = cum_ref[rows - 1 : rows, here]
        project(jnp.minimum(i + 1, chunks - 1))

        rate = rate_ref[:, at_in]
        state = jnp.zeros((states, WIDTH), F4)
        for top in range(0, rows, BLOCK):
            hist = odd if (top // BLOCK) % 2 else even
            for t in range(BLOCK):
                r = top + t
                b_now = b_ref[r * states : (r + 1) * states, :]
                b_now = jnp.concatenate([b_now] * (WIDTH // 128), axis=1)
                state = (
                    jnp.exp2(step[r : r + 1, :] * rate) * state + drive[r : r + 1, :] * b_now
                )
                hist[t * states : (t + 1) * states, :] = state.astype(BF)
            at = slice(top, top + BLOCK)
            mixed, pairs = contract(hist[...], c_ref[at, :], grad_ref[at, at_in])
            mixed_ref[at, here] += mixed
            pairs_ref[at, :] += pairs
        end_ref[:, here] = state
        send_ref[:, here] = state.astype(BF)

    pack_sums(total_ref, send_ref, folded)


def local_scan(base, width, prepared, dt_weight, dt_bias, rate, skip, conv_out, grad_out, pairs):
    rows = conv_out.shape[0]
    states = rate.shape[0]
    wide = BLOCK * states
    fresh = pairs is None
    proj, b_wide, c_wide, _ = prepared

    def body(*refs):
        refs = list(refs)
        if fresh:
            refs.insert(9, None)
        scan_kernel(base, fresh, *refs)

    ops = [proj, b_wide, c_wide, dt_weight, dt_bias, rate, skip, conv_out, grad_out]
    ops += [] if fresh else [pairs]
    work = rows * width * states
    return pl.pallas_call(
        body,
        in_specs=in_vmem(len(ops)),
        out_specs=in_vmem(6),
        out_shape=[
            jax.ShapeDtypeStruct((rows, width), F4),
            jax.ShapeDtypeStruct((rows, width), F4),
            jax.ShapeDtypeStruct((states, width), F4),
            jax.ShapeDtypeStruct((states, message_width(width, states)), BF),
            jax.ShapeDtypeStruct((1, width), F4),
            jax.ShapeDtypeStruct((rows, wide), F4),
        ],
        scratch_shapes=[
            pltpu.VMEM((rows, WIDTH), F4),
            pltpu.VMEM((rows, WIDTH), F4),
            pltpu.VMEM((rows, WIDTH), F4),
            pltpu.VMEM((states, width // states), F4),
            pltpu.VMEM((wide, WIDTH), BF),
            pltpu.VMEM((wide, WIDTH), BF),
        ],
        compiler_params=params(),
        cost_estimate=pl.CostEstimate(
            flops=600 * work, bytes_accessed=work, transcendentals=work
        ),
        name="local_scan",
    )(*ops)


def carry_kernel(
    base, scale, final,
    alt_ref, rate_ref, state_ref, cum_ref, mixed_ref, grad_ref, before_ref, local_ref, prev_ref,
    out_ref, result_ref,
    sums, rates, inits, even, odd,
):
    rows = cum_ref.shape[0]
    states = rate_ref.shape[0]
    wide = BLOCK * states
    i = pl.program_id(0)

    @pl.when(i == 0)
    def _():
        sums[...] = jnp.zeros_like(sums)

    here = chunk_at(i)
    at_in = chunk_at(i, base)
    for n in range(states):
        at = slice(n * BLOCK, (n + 1) * BLOCK)
        shape = (BLOCK, WIDTH)
        rates[at, :] = jnp.broadcast_to(rate_ref[n : n + 1, at_in], shape).astype(BF)
        inits[at, :] = jnp.broadcast_to(state_ref[n : n + 1, here], shape).astype(BF)
    for top in range(0, rows, BLOCK):
        hist = odd if (top // BLOCK) % 2 else even
        tokens = slice(top, top + BLOCK)
        cum = cum_ref[tokens, here].astype(BF)
        grad = grad_ref[tokens, at_in]
        for n in range(states):
            at = slice(n * BLOCK, (n + 1) * BLOCK)
            now = jnp.exp2(cum * rates[at, :]) * inits[at, :]
            hist[at, :] = now
            pairs = now * grad
            parts = [pairs[:, k : k + 128] for k in range(0, WIDTH, 128)]
            while len(parts) > 1:
                parts = [a + b for a, b in zip(parts[::2], parts[1::2])]
            sums[n, tokens, :] += parts[0].astype(F4)
        mixed = jnp.dot(alt_ref[tokens, :], hist[...], preferred_element_type=F4)
        out_ref[tokens, :] = (mixed_ref[tokens, here] + mixed).astype(BF)

    @pl.when(i == pl.num_programs(0) - 1)
    def _():
        ones = jnp.ones((8, 256), BF)
        if final:
            lane = wide_iota((rows, wide), 1)
            row = wide_iota((rows, wide), 0) % BLOCK
            by_token = jnp.where(lane // states == row, local_ref[...], 0.0)
            pick = wide_iota((states, wide), 1) % states == wide_iota((states, wide), 0)
            result_ref[...] = before_ref[...] + lax.dot_general(
                pick.astype(F4), by_token, NT,
                preferred_element_type=F4, precision=lax.Precision.HIGHEST,
            )
        else:
            result_ref[...] = jnp.zeros_like(result_ref)
        for n in range(states):
            high = sums[n].astype(BF)
            low = (sums[n] - high.astype(F4)).astype(BF)
            both = jnp.concatenate([high, low], axis=1)
            line = lax.dot_general(ones, both, NT, preferred_element_type=F4)
            result_ref[n : n + 1, :] += line[0:1, :]
        if final:
            result_ref[...] = result_ref[...] * scale


def add_carry(base, scale, alt, rate, incoming, cum, mixed, grad_out, before, local, prev):
    rows, width = cum.shape
    states, channels = rate.shape
    wide = BLOCK * states
    final = local is not None
    ops = [alt, rate, incoming, cum, mixed, grad_out]
    specs = in_vmem(6)
    if final:
        ops += [before, local, prev]
        specs += in_vmem(2) + [pl.BlockSpec(memory_space=pl.ANY)]

    def body(*refs):
        refs = list(refs)
        if not final:
            refs[6:6] = [None] * 3
        carry_kernel(base, scale, final, *refs)

    work = rows * width * states
    return pl.pallas_call(
        body,
        grid=(width // WIDTH,),
        in_specs=specs,
        out_specs=[
            pl.BlockSpec((rows, WIDTH), lambda i: (0, i + base)),
            whole(states, rows),
        ],
        out_shape=[
            jax.ShapeDtypeStruct((rows, channels), BF),
            jax.ShapeDtypeStruct((states, rows), F4),
        ],
        scratch_shapes=[
            pltpu.VMEM((states, rows, 128), F4),
            pltpu.VMEM((wide, WIDTH), BF),
            pltpu.VMEM((wide, WIDTH), BF),
            pltpu.VMEM((wide, WIDTH), BF),
            pltpu.VMEM((wide, WIDTH), BF),
        ],
        input_output_aliases={len(ops) - 1: 0} if final else {},
        compiler_params=params(),
        cost_estimate=pl.CostEstimate(
            flops=300 * work, bytes_accessed=work, transcendentals=work
        ),
        name="add_carry",
    )(*ops)


def merge_kernel(
    base, bit, last, rate_ref, end_ref, total_ref, got_ref, pre_ref, psum_ref, *refs
):
    *outs, osum_ref, folded = refs
    later = (lax.axis_index("seq") & bit) != 0
    unpack_sums(got_ref, osum_ref, folded)
    for i in range(end_ref.shape[1] // WIDTH):
        at = slice(i * WIDTH, (i + 1) * WIDTH)
        rate = rate_ref[:, (base + i) * WIDTH : (base + i + 1) * WIDTH]
        fade = lambda s: jnp.exp2(rate * s)
        other = got_ref[:, at].astype(F4)
        prefix, before = pre_ref[:, at], psum_ref[:, at]
        outs[0][:, at] = jnp.where(later, prefix + fade(before) * other, prefix)
        if not last:
            total, osum, end = total_ref[:, at], osum_ref[:, at], end_ref[:, at]
            outs[1][:, at] = jnp.where(later, before + osum, before)
            first = jnp.where(later, other, end)
            second = jnp.where(later, end, other)
            end = second + fade(jnp.where(later, total, osum)) * first
            outs[2][:, at] = end
            outs[3][:, at] = end.astype(BF)
            outs[4][:, at] = total + osum
    if not last:
        pack_sums(outs[4], outs[3], folded)


def merge(base, bit, last, rate, end, total, got, prefix, prefix_sum):
    states, width = end.shape
    outs = [jax.ShapeDtypeStruct((states, width), F4)]
    if not last:
        outs += [
            jax.ShapeDtypeStruct((1, width), F4),
            jax.ShapeDtypeStruct((states, width), F4),
            jax.ShapeDtypeStruct(got.shape, BF),
            jax.ShapeDtypeStruct((1, width), F4),
        ]

    def body(*refs):
        merge_kernel(base, bit, last, *refs)

    return pl.pallas_call(
        body,
        in_specs=in_vmem(6),
        out_specs=in_vmem(len(outs)),
        out_shape=outs,
        scratch_shapes=[
            pltpu.VMEM((1, width), F4),
            pltpu.VMEM((states, width // states), F4),
        ],
        compiler_params=params(),
        name="merge",
    )(rate, end, total, got, prefix, prefix_sum)


def weight_first(parts, conv_out, count):
    states, rows = parts[0].shape
    share = conv_out.shape[1] // count
    many = len(parts)

    def body(*refs):
        conv_ref, out_ref = refs[many:]
        grad_c = refs[0][...]
        for r in refs[1:many]:
            grad_c = grad_c + r[...]
        grad_c = grad_c.astype(BF)
        for j in range(count):
            block = conv_ref[:, j * share : (j + 1) * share]
            out_ref[j] = jnp.dot(grad_c, block, preferred_element_type=F4).astype(BF)

    return pl.pallas_call(
        body,
        in_specs=in_vmem(many + 1),
        out_specs=pl.BlockSpec(memory_space=pltpu.VMEM),
        out_shape=jax.ShapeDtypeStruct((count, states, share), BF),
        compiler_params=params(),
        name="weight_first",
    )(*parts, conv_out)


def weight_gradient(parts, conv_out):
    count = lax.axis_size("seq")
    states = parts[0].shape[0]
    share = conv_out.shape[1] // count
    if share % 128 == 0:
        weight = weight_first(parts, conv_out, count)
    else:
        grad_c = sum(parts[1:], parts[0]).astype(BF)
        weight = jnp.dot(grad_c, conv_out, preferred_element_type=F4).astype(BF)
        weight = weight.reshape(states, count, share).transpose(1, 0, 2)
    weight = lax.all_to_all(weight, "seq", 0, 0)
    return jnp.sum(weight.astype(F4), axis=0).T


def exchange(base, bit, rate, held):
    end, send, total, prefix, prefix_sum = held
    last = 2 * bit >= lax.axis_size("seq")
    got = swap(send, "seq", bit)
    outs = merge(base, bit, last, rate, end, total, got, prefix, prefix_sum)
    if last:
        return outs[0]
    prefix, prefix_sum, end, send, total = outs
    return end, send, total, prefix, prefix_sum


def on_device(
    conv_in,
    conv_weight,
    conv_bias,
    proj_weight,
    dt_weight,
    dt_bias,
    decay_rate,
    skip_gain,
    grad_out,
):
    rows, channels = conv_in.shape
    taps = conv_weight.shape[0]
    rank = dt_weight.shape[0]
    states = decay_rate.shape[0]
    count = lax.axis_size("seq")
    tp = lax.axis_size("tp")
    rim_rows = 8 * -(-(taps - 1) // 8)
    edge = conv_in[rows - rim_rows :]
    rims = [
        lax.ppermute(edge, "seq", [p for i in range(k, count - 1, 2) for p in ((i, i + 1), (i + 1, i))])
        for k in range(2)
    ]
    x, w, bias, weight_t = fetch(conv_in, conv_weight, conv_bias[None], proj_weight.T)
    rate = decay_rate * (-LOG2E)
    conv_out, part = conv_project(x, rims, w, bias, weight_t)
    mine = add_first(part, swap(part, "tp", 1), rank)
    other = swap(mine, "tp", 2)
    bit = 4
    while bit < tp:
        mine = add_later(mine, other, part.shape[1], rank)
        other = swap(mine, "tp", bit)
        bit *= 2
    prepared = prepare(mine, other, rank, states)

    width = channels // 2
    bases = (0, width // WIDTH)
    pairs = None
    local, held = [], []
    for base in bases:
        mixed, cum, end, send, total, pairs = local_scan(
            base, width, prepared, dt_weight, dt_bias[None], rate, skip_gain[None],
            conv_out, grad_out, pairs,
        )
        local.append((cum, mixed))
        held.append((end, send, total, jnp.zeros_like(end), jnp.zeros_like(total)))
    bit = 1
    while bit < count:
        held = [exchange(base, bit, rate, h) for base, h in zip(bases, held)]
        bit *= 2

    scale = 1.0 / (rows * count)
    shared = (scale, prepared[3], rate)
    mixed, more = add_carry(bases[0], *shared, held[0], *local[0], grad_out, None, None, None)
    mixed, grad_c = add_carry(bases[1], *shared, held[1], *local[1], grad_out, more, pairs, mixed)
    parts = [grad_c] + [swap(grad_c, "tp", k) for k in range(1, tp)]
    weight_grad = weight_gradient(parts, conv_out)
    return (mixed, weight_grad[None])


def solution(mesh):
    return jax.shard_map(
        on_device,
        mesh=mesh,
        in_specs=(
            P("seq", "tp"),
            P(None, "tp"),
            P("tp"),
            P("tp", None),
            P(None, "tp"),
            P("tp"),
            P(None, "tp"),
            P("tp"),
            P("seq", "tp"),
        ),
        out_specs=(P("seq", "tp"), P("tp", "seq", None)),
        check_vma=False,
    )
```

```python
import math

import jax
import jax.numpy as jnp
from jax import lax
from jax.experimental import pallas as pl
from jax.experimental.pallas import tpu as pltpu
from jax.sharding import PartitionSpec as P

LOG2E = math.log2(math.e)
BLOCK = 16
WIDTH = 512
BF = jnp.bfloat16
F4 = jnp.float32
NT = (((1,), (1,)), ((), ()))
TN = (((0,), (0,)), ((), ()))


def swap(a, axis, bit):
    count = lax.axis_size(axis)
    return lax.ppermute(a, axis, [(i, i ^ bit) for i in range(count)])


def params(limit=12 << 20):
    return pltpu.CompilerParams(vmem_limit_bytes=limit)


def cols(rows):
    return pl.BlockSpec((rows, WIDTH), lambda i: (0, i))


def whole(rows, lanes):
    return pl.BlockSpec((rows, lanes), lambda i: (0, 0))


def chunk_at(i, base=0):
    return pl.ds(pl.multiple_of((base + i) * WIDTH, WIDTH), WIDTH)


def conv_rows(ext, j, weights, bias, tops, base):
    for top in tops:
        acc = bias
        for tap in range(weights.shape[0]):
            at = base + top + tap
            acc = acc + weights[tap : tap + 1, :] * ext[j, at : at + BLOCK, :]
        half = 0.5 * acc
        yield top, (half + half * jnp.tanh(half)).astype(BF)


def conv_body_kernel(
    x_hbm, w_hbm, bias_hbm, proj_hbm, x_ref, w_ref, bias_ref, proj_ref, out_ref,
    ext, sems, x_sems,
):
    rows, channels = x_ref.shape
    chunks = channels // WIDTH

    def x_copy(i):
        at = chunk_at(i)
        return pltpu.make_async_copy(x_hbm.at[:, at], x_ref.at[:, at], x_sems.at[i])

    w_copy = pltpu.make_async_copy(w_hbm, w_ref, sems.at[0])
    bias_copy = pltpu.make_async_copy(bias_hbm, bias_ref, sems.at[1])
    proj_copy = pltpu.make_async_copy(proj_hbm, proj_ref, sems.at[2])
    w_copy.start()
    bias_copy.start()
    for i in range(chunks):
        x_copy(i).start()
    proj_copy.start()
    w_copy.wait()
    bias_copy.wait()

    @pl.loop(0, chunks)
    def _(i):
        x_copy(i).wait()
        for j in range(WIDTH // 128):
            lanes = pl.ds(pl.multiple_of(i * WIDTH + j * 128, 128), 128)
            ext[j] = x_ref[:, lanes].astype(F4)
            base = 1 - w_ref.shape[0]
            tops = range(BLOCK, rows, BLOCK)
            for top, out in conv_rows(ext, j, w_ref[:, lanes], bias_ref[:, lanes], tops, base):
                out_ref[top : top + BLOCK, lanes] = out
            out_ref[0:BLOCK, lanes] = jnp.zeros((BLOCK, 128), BF)

    proj_copy.wait()


def conv_body(conv_in, conv_weight, conv_bias, proj_weight_t):
    arrays = (conv_in, conv_weight, conv_bias, proj_weight_t)
    rows, channels = conv_in.shape
    moved = 2 * sum(a.size * a.dtype.itemsize for a in arrays)
    return pl.pallas_call(
        conv_body_kernel,
        in_specs=[pl.BlockSpec(memory_space=pltpu.HBM)] * 4,
        out_specs=in_vmem(5),
        out_shape=[pltpu.VMEM(a.shape, a.dtype) for a in arrays]
        + [pltpu.VMEM((rows, channels), BF)],
        scratch_shapes=[
            pltpu.VMEM((WIDTH // 128, rows, 128), F4),
            pltpu.SemaphoreType.DMA((3,)),
            pltpu.SemaphoreType.DMA((channels // WIDTH,)),
        ],
        compiler_params=params(),
        cost_estimate=pl.CostEstimate(
            flops=20 * rows * channels, bytes_accessed=moved, transcendentals=rows * channels
        ),
        name="conv_body",
    )(*[in_hbm(a) for a in arrays])


def conv_kernel(
    x_ref, odd_ref, even_ref, w_ref, bias_ref, proj_ref, conv_ref, out_ref, part_ref, ext
):
    rows, channels = out_ref.shape
    rim = odd_ref.shape[0]
    base = rim - (w_ref.shape[0] - 1)
    odd = (lax.axis_index("seq") & 1) != 0
    part_ref[...] = jnp.zeros_like(part_ref)

    @pl.loop(0, channels // WIDTH)
    def _(i):
        for j in range(WIDTH // 128):
            lanes = pl.ds(pl.multiple_of(i * WIDTH + j * 128, 128), 128)
            ext[j, 0:rim, :] = jnp.where(
                odd, odd_ref[:, lanes].astype(F4), even_ref[:, lanes].astype(F4)
            )
            ext[j, rim:, :] = x_ref[0:BLOCK, lanes].astype(F4)
            for top, out in conv_rows(ext, j, w_ref[:, lanes], bias_ref[:, lanes], (0,), base):
                out_ref[0:BLOCK, lanes] = out
        at = chunk_at(i)
        part_ref[...] += lax.dot_general(
            out_ref[:, at], proj_ref[:, at], NT, preferred_element_type=F4
        )


def conv_project(x, rims, w, bias, proj_weight_t, conv_out):
    rows, channels = conv_out.shape
    wide = proj_weight_t.shape[0]
    rim = rims[0].shape[0]
    return pl.pallas_call(
        conv_kernel,
        in_specs=in_vmem(7),
        out_specs=in_vmem(2),
        out_shape=[
            jax.ShapeDtypeStruct((rows, channels), BF),
            jax.ShapeDtypeStruct((rows, wide), F4),
        ],
        scratch_shapes=[pltpu.VMEM((WIDTH // 128, BLOCK + rim, 128), F4)],
        input_output_aliases={6: 0},
        compiler_params=params(),
        name="conv_project",
    )(x, *rims, w, bias, proj_weight_t, conv_out)


def in_hbm(a):
    return pltpu.with_memory_space_constraint(a, pltpu.HBM)


def in_vmem(count):
    return [pl.BlockSpec(memory_space=pltpu.VMEM)] * count


def split_sum(total, rank, out_ref):
    wide = total.shape[1]
    high = total.astype(BF)
    out_ref[:, :wide] = high
    out_ref[:, wide:] = (total[:, rank:] - high[:, rank:].astype(F4)).astype(BF)


def joined(ref, wide, rank):
    high = ref[:, :wide].astype(F4)
    return high[:, :rank], high[:, rank:] + ref[:, wide:].astype(F4)


def add_first(part, other, rank):
    rows, wide = part.shape

    def body(a_ref, b_ref, out_ref):
        split_sum(a_ref[...] + b_ref[...], rank, out_ref)

    return pl.pallas_call(
        body,
        in_specs=in_vmem(2),
        out_specs=pl.BlockSpec(memory_space=pltpu.VMEM),
        out_shape=jax.ShapeDtypeStruct((rows, 2 * wide - rank), BF),
        compiler_params=params(),
        name="add_first",
    )(part, other)


def add_later(mine, other, wide, rank):
    def body(a_ref, b_ref, out_ref):
        a_low, a_high = joined(a_ref, wide, rank)
        b_low, b_high = joined(b_ref, wide, rank)
        total = jnp.concatenate([a_low + b_low, a_high + b_high], axis=1)
        split_sum(total, rank, out_ref)

    return pl.pallas_call(
        body,
        in_specs=in_vmem(2),
        out_specs=pl.BlockSpec(memory_space=pltpu.VMEM),
        out_shape=jax.ShapeDtypeStruct(mine.shape, BF),
        compiler_params=params(),
        name="add_later",
    )(mine, other)


def softplus(x):
    u = jnp.exp(-jnp.abs(x))
    small = u * (1.0 - u * (0.5 - u * (1.0 / 3.0)))
    return jnp.maximum(x, 0.0) + jnp.where(u < 0.0078125, small, jnp.log(1.0 + u))


def wide_iota(shape, axis):
    return lax.broadcasted_iota(jnp.int32, shape, axis)


def contract(block, c_now, grad_now):
    mixed = jnp.dot(c_now, block, preferred_element_type=F4)
    pairs = lax.dot_general(grad_now, block, NT, preferred_element_type=F4)
    return mixed, pairs


def prepare_kernel(mine_ref, other_ref, proj_ref, b_ref, c_ref, alt_ref):
    rows, rank = proj_ref.shape
    wide = c_ref.shape[1]
    states = wide // BLOCK
    a_low, a_high = joined(mine_ref, rank + 2 * states, rank)
    b_low, b_high = joined(other_ref, rank + 2 * states, rank)
    proj_ref[...] = (a_low + b_low).astype(BF)
    ends = (a_high + b_high).astype(BF)
    lane = wide_iota((states, wide), 1)
    row = wide_iota((states, wide), 0)
    by_token = (lane % states == row).astype(BF)
    by_state = (lane // BLOCK == row).astype(BF)
    lane = wide_iota((rows, wide), 1)
    row = wide_iota((rows, wide), 0) % BLOCK
    c_mat = ends[:, states:]
    tiled = jnp.dot(c_mat, by_token, preferred_element_type=F4)
    c_ref[...] = jnp.where(lane // states == row, tiled, 0.0).astype(BF)
    tiled = jnp.dot(c_mat, by_state, preferred_element_type=F4)
    alt_ref[...] = jnp.where(lane % BLOCK == row, tiled, 0.0).astype(BF)
    tiled = jnp.dot(ends[:, :states], by_token, preferred_element_type=F4)
    b_diag = jnp.where(lane // states == row, tiled, 0.0).astype(BF)
    ones = jnp.ones((BLOCK, 128), BF)
    for top in range(0, rows, BLOCK):
        b_ref[top * states : (top + BLOCK) * states, :] = lax.dot_general(
            b_diag[top : top + BLOCK, :], ones, TN, preferred_element_type=F4
        )


def prepare(mine, other, rank, states):
    rows = mine.shape[0]
    wide = BLOCK * states
    return pl.pallas_call(
        prepare_kernel,
        in_specs=in_vmem(2),
        out_specs=in_vmem(4),
        out_shape=[
            jax.ShapeDtypeStruct((rows, rank), BF),
            jax.ShapeDtypeStruct((rows * states, 128), F4),
            jax.ShapeDtypeStruct((rows, wide), BF),
            jax.ShapeDtypeStruct((rows, wide), BF),
        ],
        compiler_params=params(),
        name="prepare",
    )(mine, other)


def pack_sums(total_ref, send_ref, folded):
    states, per = folded.shape
    width = states * per
    for n in range(states):
        folded[n : n + 1, :] = total_ref[:, n * per : (n + 1) * per]
    high = folded[...].astype(BF)
    send_ref[:, width : width + per] = high
    send_ref[:, width + per :] = (folded[...] - high.astype(F4)).astype(BF)


def unpack_sums(got_ref, sum_ref, folded):
    states, per = folded.shape
    width = states * per
    folded[...] = got_ref[:, width : width + per].astype(F4) + got_ref[:, width + per :].astype(F4)
    for n in range(states):
        sum_ref[:, n * per : (n + 1) * per] = folded[n : n + 1, :]


def message_width(width, states):
    return width + 2 * (width // states)


def scan_kernel(
    base, fresh,
    proj_ref, b_ref, c_ref, dtw_ref, dtb_ref, rate_ref, skip_ref, conv_ref, grad_ref, pairs_in,
    mixed_ref, cum_ref, end_ref, send_ref, total_ref, pairs_ref,
    raw, step, drive, folded, even, odd,
):
    rows = conv_ref.shape[0]
    states = rate_ref.shape[0]
    chunks = mixed_ref.shape[1] // WIDTH
    pairs_ref[...] = jnp.zeros_like(pairs_ref) if fresh else pairs_in[...]
    tri = (wide_iota((rows, rows), 0) >= wide_iota((rows, rows), 1)).astype(BF)

    def project(i):
        raw[...] = jnp.dot(proj_ref[...], dtw_ref[:, chunk_at(i, base)], preferred_element_type=F4)

    project(0)

    @pl.loop(0, chunks)
    def _(i):
        here = chunk_at(i)
        at_in = chunk_at(i, base)
        bias = dtb_ref[:, at_in]
        skip = skip_ref[:, at_in]
        rounded = []
        for top in range(0, rows, BLOCK):
            at = slice(top, top + BLOCK)
            now = softplus(raw[at, :] + bias)
            step[at, :] = now
            conv = conv_ref[at, at_in].astype(F4)
            drive[at, :] = now * conv
            mixed_ref[at, here] = skip * conv
            rounded.append(now.astype(BF))
        cum_ref[:, here] = jnp.dot(
            tri, jnp.concatenate(rounded, axis=0), preferred_element_type=F4
        )
        total_ref[:, here] = cum_ref[rows - 1 : rows, here]
        project(jnp.minimum(i + 1, chunks - 1))

        rate = rate_ref[:, at_in]
        state = jnp.zeros((states, WIDTH), F4)
        for top in range(0, rows, BLOCK):
            hist = odd if (top // BLOCK) % 2 else even
            for t in range(BLOCK):
                r = top + t
                b_now = b_ref[r * states : (r + 1) * states, :]
                b_now = jnp.concatenate([b_now] * (WIDTH // 128), axis=1)
                state = (
                    jnp.exp2(step[r : r + 1, :] * rate) * state + drive[r : r + 1, :] * b_now
                )
                hist[t * states : (t + 1) * states, :] = state.astype(BF)
            at = slice(top, top + BLOCK)
            mixed, pairs = contract(hist[...], c_ref[at, :], grad_ref[at, at_in])
            mixed_ref[at, here] += mixed
            pairs_ref[at, :] += pairs
        end_ref[:, here] = state
        send_ref[:, here] = state.astype(BF)

    pack_sums(total_ref, send_ref, folded)


def local_scan(base, width, prepared, dt_weight, dt_bias, rate, skip, conv_out, grad_out, pairs):
    rows = conv_out.shape[0]
    states = rate.shape[0]
    wide = BLOCK * states
    fresh = pairs is None
    proj, b_wide, c_wide, _ = prepared

    def body(*refs):
        refs = list(refs)
        if fresh:
            refs.insert(9, None)
        scan_kernel(base, fresh, *refs)

    ops = [proj, b_wide, c_wide, dt_weight, dt_bias, rate, skip, conv_out, grad_out]
    ops += [] if fresh else [pairs]
    work = rows * width * states
    return pl.pallas_call(
        body,
        in_specs=in_vmem(len(ops)),
        out_specs=in_vmem(6),
        out_shape=[
            jax.ShapeDtypeStruct((rows, width), F4),
            jax.ShapeDtypeStruct((rows, width), F4),
            jax.ShapeDtypeStruct((states, width), F4),
            jax.ShapeDtypeStruct((states, message_width(width, states)), BF),
            jax.ShapeDtypeStruct((1, width), F4),
            jax.ShapeDtypeStruct((rows, wide), F4),
        ],
        scratch_shapes=[
            pltpu.VMEM((rows, WIDTH), F4),
            pltpu.VMEM((rows, WIDTH), F4),
            pltpu.VMEM((rows, WIDTH), F4),
            pltpu.VMEM((states, width // states), F4),
            pltpu.VMEM((wide, WIDTH), BF),
            pltpu.VMEM((wide, WIDTH), BF),
        ],
        compiler_params=params(),
        cost_estimate=pl.CostEstimate(
            flops=600 * work, bytes_accessed=work, transcendentals=work
        ),
        name="local_scan",
    )(*ops)


def carry_kernel(
    base, scale, final,
    alt_ref, rate_ref, state_ref, cum_ref, mixed_ref, grad_ref, before_ref, local_ref, prev_ref,
    out_ref, result_ref,
    sums, rates, inits, even, odd,
):
    rows = cum_ref.shape[0]
    states = rate_ref.shape[0]
    wide = BLOCK * states
    i = pl.program_id(0)

    @pl.when(i == 0)
    def _():
        sums[...] = jnp.zeros_like(sums)

    here = chunk_at(i)
    at_in = chunk_at(i, base)
    for n in range(states):
        at = slice(n * BLOCK, (n + 1) * BLOCK)
        shape = (BLOCK, WIDTH)
        rates[at, :] = jnp.broadcast_to(rate_ref[n : n + 1, at_in], shape).astype(BF)
        inits[at, :] = jnp.broadcast_to(state_ref[n : n + 1, here], shape).astype(BF)
    for top in range(0, rows, BLOCK):
        hist = odd if (top // BLOCK) % 2 else even
        tokens = slice(top, top + BLOCK)
        cum = cum_ref[tokens, here].astype(BF)
        grad = grad_ref[tokens, at_in]
        for n in range(states):
            at = slice(n * BLOCK, (n + 1) * BLOCK)
            now = jnp.exp2(cum * rates[at, :]) * inits[at, :]
            hist[at, :] = now
            pairs = now * grad
            parts = [pairs[:, k : k + 128] for k in range(0, WIDTH, 128)]
            low = (parts[0] + parts[1]).astype(F4)
            sums[n, tokens, :] += low + (parts[2] + parts[3]).astype(F4)
        mixed = jnp.dot(alt_ref[tokens, :], hist[...], preferred_element_type=F4)
        out_ref[tokens, :] = (mixed_ref[tokens, here] + mixed).astype(BF)

    @pl.when(i == pl.num_programs(0) - 1)
    def _():
        ones = jnp.ones((8, 256), BF)
        if final:
            lane = wide_iota((rows, wide), 1)
            row = wide_iota((rows, wide), 0) % BLOCK
            by_token = jnp.where(lane // states == row, local_ref[...], 0.0)
            pick = wide_iota((states, wide), 1) % states == wide_iota((states, wide), 0)
            result_ref[...] = before_ref[...] + lax.dot_general(
                pick.astype(F4), by_token, NT,
                preferred_element_type=F4, precision=lax.Precision.HIGHEST,
            )
        else:
            result_ref[...] = jnp.zeros_like(result_ref)
        for n in range(states):
            high = sums[n].astype(BF)
            low = (sums[n] - high.astype(F4)).astype(BF)
            both = jnp.concatenate([high, low], axis=1)
            line = lax.dot_general(ones, both, NT, preferred_element_type=F4)
            result_ref[n : n + 1, :] += line[0:1, :]
        if final:
            result_ref[...] = result_ref[...] * scale


def add_carry(base, scale, alt, rate, incoming, cum, mixed, grad_out, before, local, prev):
    rows, width = cum.shape
    states, channels = rate.shape
    wide = BLOCK * states
    final = local is not None
    ops = [alt, rate, incoming, cum, mixed, grad_out]
    specs = in_vmem(6)
    if final:
        ops += [before, local, prev]
        specs += in_vmem(2) + [pl.BlockSpec(memory_space=pl.ANY)]

    def body(*refs):
        refs = list(refs)
        if not final:
            refs[6:6] = [None] * 3
        carry_kernel(base, scale, final, *refs)

    work = rows * width * states
    return pl.pallas_call(
        body,
        grid=(width // WIDTH,),
        in_specs=specs,
        out_specs=[
            pl.BlockSpec((rows, WIDTH), lambda i: (0, i + base)),
            whole(states, rows),
        ],
        out_shape=[
            jax.ShapeDtypeStruct((rows, channels), BF),
            jax.ShapeDtypeStruct((states, rows), F4),
        ],
        scratch_shapes=[
            pltpu.VMEM((states, rows, 128), F4),
            pltpu.VMEM((wide, WIDTH), BF),
            pltpu.VMEM((wide, WIDTH), BF),
            pltpu.VMEM((wide, WIDTH), BF),
            pltpu.VMEM((wide, WIDTH), BF),
        ],
        input_output_aliases={len(ops) - 1: 0} if final else {},
        compiler_params=params(),
        cost_estimate=pl.CostEstimate(
            flops=300 * work, bytes_accessed=work, transcendentals=work
        ),
        name="add_carry",
    )(*ops)


def merge_kernel(
    base, bit, last, rate_ref, end_ref, total_ref, got_ref, pre_ref, psum_ref, *refs
):
    *outs, osum_ref, folded = refs
    later = (lax.axis_index("seq") & bit) != 0
    unpack_sums(got_ref, osum_ref, folded)
    for i in range(end_ref.shape[1] // WIDTH):
        at = slice(i * WIDTH, (i + 1) * WIDTH)
        rate = rate_ref[:, (base + i) * WIDTH : (base + i + 1) * WIDTH]
        fade = lambda s: jnp.exp2(rate * s)
        other = got_ref[:, at].astype(F4)
        prefix, before = pre_ref[:, at], psum_ref[:, at]
        outs[0][:, at] = jnp.where(later, prefix + fade(before) * other, prefix)
        if not last:
            total, osum, end = total_ref[:, at], osum_ref[:, at], end_ref[:, at]
            outs[1][:, at] = jnp.where(later, before + osum, before)
            first = jnp.where(later, other, end)
            second = jnp.where(later, end, other)
            end = second + fade(jnp.where(later, total, osum)) * first
            outs[2][:, at] = end
            outs[3][:, at] = end.astype(BF)
            outs[4][:, at] = total + osum
    if not last:
        pack_sums(outs[4], outs[3], folded)


def merge(base, bit, last, rate, end, total, got, prefix, prefix_sum):
    states, width = end.shape
    outs = [jax.ShapeDtypeStruct((states, width), F4)]
    if not last:
        outs += [
            jax.ShapeDtypeStruct((1, width), F4),
            jax.ShapeDtypeStruct((states, width), F4),
            jax.ShapeDtypeStruct(got.shape, BF),
            jax.ShapeDtypeStruct((1, width), F4),
        ]

    def body(*refs):
        merge_kernel(base, bit, last, *refs)

    return pl.pallas_call(
        body,
        in_specs=in_vmem(6),
        out_specs=in_vmem(len(outs)),
        out_shape=outs,
        scratch_shapes=[
            pltpu.VMEM((1, width), F4),
            pltpu.VMEM((states, width // states), F4),
        ],
        compiler_params=params(),
        name="merge",
    )(rate, end, total, got, prefix, prefix_sum)


def weight_first(parts, conv_out, count):
    states, rows = parts[0].shape
    share = conv_out.shape[1] // count
    many = len(parts)

    def body(*refs):
        conv_ref, out_ref = refs[many:]
        grad_c = refs[0][...]
        for r in refs[1:many]:
            grad_c = grad_c + r[...]
        high = grad_c.astype(BF)
        low = (grad_c - high.astype(F4)).astype(BF)
        both = jnp.concatenate([high, low], axis=0)
        for j in range(count):
            block = conv_ref[:, j * share : (j + 1) * share]
            out = jnp.dot(both, block, preferred_element_type=F4)
            out_ref[j] = (out[:states, :] + out[states:, :]).astype(BF)

    return pl.pallas_call(
        body,
        in_specs=in_vmem(many + 1),
        out_specs=pl.BlockSpec(memory_space=pltpu.VMEM),
        out_shape=jax.ShapeDtypeStruct((count, states, share), BF),
        compiler_params=params(),
        name="weight_first",
    )(*parts, conv_out)


def weight_gradient(parts, conv_out):
    count = lax.axis_size("seq")
    states = parts[0].shape[0]
    share = conv_out.shape[1] // count
    if share % 128 == 0:
        weight = weight_first(parts, conv_out, count)
    else:
        grad_c = sum(parts[1:], parts[0]).astype(BF)
        weight = jnp.dot(grad_c, conv_out, preferred_element_type=F4).astype(BF)
        weight = weight.reshape(states, count, share).transpose(1, 0, 2)
    weight = lax.all_to_all(weight, "seq", 0, 0)
    return jnp.sum(weight.astype(F4), axis=0).T


def exchange(base, bit, rate, held):
    end, send, total, prefix, prefix_sum = held
    last = 2 * bit >= lax.axis_size("seq")
    got = swap(send, "seq", bit)
    outs = merge(base, bit, last, rate, end, total, got, prefix, prefix_sum)
    if last:
        return outs[0]
    prefix, prefix_sum, end, send, total = outs
    return end, send, total, prefix, prefix_sum


def on_device(
    conv_in,
    conv_weight,
    conv_bias,
    proj_weight,
    dt_weight,
    dt_bias,
    decay_rate,
    skip_gain,
    grad_out,
):
    rows, channels = conv_in.shape
    taps = conv_weight.shape[0]
    rank = dt_weight.shape[0]
    states = decay_rate.shape[0]
    count = lax.axis_size("seq")
    tp = lax.axis_size("tp")
    rim_rows = 8 * -(-(taps - 1) // 8)
    edge = conv_in[rows - rim_rows :]
    rims = [
        lax.ppermute(edge, "seq", [p for i in range(k, count - 1, 2) for p in ((i, i + 1), (i + 1, i))])
        for k in range(2)
    ]
    x, w, bias, weight_t, conv_out = conv_body(
        conv_in, conv_weight, conv_bias[None], proj_weight.T
    )
    rate = decay_rate * (-LOG2E)
    conv_out, part = conv_project(x, rims, w, bias, weight_t, conv_out)
    mine = add_first(part, swap(part, "tp", 1), rank)
    other = swap(mine, "tp", 2)
    bit = 4
    while bit < tp:
        mine = add_later(mine, other, part.shape[1], rank)
        other = swap(mine, "tp", bit)
        bit *= 2
    prepared = prepare(mine, other, rank, states)

    width = channels // 2
    bases = (0, width // WIDTH)
    pairs = None
    local, held = [], []
    for base in bases:
        mixed, cum, end, send, total, pairs = local_scan(
            base, width, prepared, dt_weight, dt_bias[None], rate, skip_gain[None],
            conv_out, grad_out, pairs,
        )
        local.append((cum, mixed))
        held.append((end, send, total, jnp.zeros_like(end), jnp.zeros_like(total)))
    bit = 1
    while bit < count:
        held = [exchange(base, bit, rate, h) for base, h in zip(bases, held)]
        bit *= 2

    scale = 1.0 / (rows * count)
    shared = (scale, prepared[3], rate)
    mixed, more = add_carry(bases[0], *shared, held[0], *local[0], grad_out, None, None, None)
    mixed, grad_c = add_carry(bases[1], *shared, held[1], *local[1], grad_out, more, pairs, mixed)
    parts = [grad_c] + [swap(grad_c, "tp", k) for k in range(1, tp)]
    weight_grad = weight_gradient(parts, conv_out)
    return (mixed, weight_grad[None])


def solution(mesh):
    return jax.shard_map(
        on_device,
        mesh=mesh,
        in_specs=(
            P("seq", "tp"),
            P(None, "tp"),
            P("tp"),
            P("tp", None),
            P(None, "tp"),
            P("tp"),
            P(None, "tp"),
            P("tp"),
            P("seq", "tp"),
        ),
        out_specs=(P("seq", "tp"), P("tp", "seq", None)),
        check_vma=False,
    )
```

```python
import math

import jax
import jax.numpy as jnp
from jax import lax
from jax.experimental import pallas as pl
from jax.experimental.pallas import tpu as pltpu
from jax.sharding import PartitionSpec as P

LOG2E = math.log2(math.e)
BLOCK = 16
WIDTH = 512
BF = jnp.bfloat16
F4 = jnp.float32
NT = (((1,), (1,)), ((), ()))
TN = (((0,), (0,)), ((), ()))


def swap(a, axis, bit):
    count = lax.axis_size(axis)
    return lax.ppermute(a, axis, [(i, i ^ bit) for i in range(count)])


def params(limit=12 << 20):
    return pltpu.CompilerParams(vmem_limit_bytes=limit)


def cols(rows):
    return pl.BlockSpec((rows, WIDTH), lambda i: (0, i))


def whole(rows, lanes):
    return pl.BlockSpec((rows, lanes), lambda i: (0, 0))


def chunk_at(i, base=0):
    return pl.ds(pl.multiple_of((base + i) * WIDTH, WIDTH), WIDTH)


def conv_rows(ext, j, weights, bias, tops, base):
    for top in tops:
        acc = bias
        for tap in range(weights.shape[0]):
            at = base + top + tap
            acc = acc + weights[tap : tap + 1, :] * ext[j, at : at + BLOCK, :]
        half = 0.5 * acc
        yield top, (half + half * jnp.tanh(half)).astype(BF)


def conv_body_kernel(
    x_hbm, w_hbm, bias_hbm, proj_hbm, x_ref, w_ref, bias_ref, proj_ref, out_ref,
    ext, sems, x_sems,
):
    rows, channels = x_ref.shape
    chunks = channels // WIDTH

    def x_copy(i):
        at = chunk_at(i)
        return pltpu.make_async_copy(x_hbm.at[:, at], x_ref.at[:, at], x_sems.at[i])

    w_copy = pltpu.make_async_copy(w_hbm, w_ref, sems.at[0])
    bias_copy = pltpu.make_async_copy(bias_hbm, bias_ref, sems.at[1])
    proj_copy = pltpu.make_async_copy(proj_hbm, proj_ref, sems.at[2])
    w_copy.start()
    bias_copy.start()
    for i in range(chunks):
        x_copy(i).start()
    proj_copy.start()
    w_copy.wait()
    bias_copy.wait()

    @pl.loop(0, chunks)
    def _(i):
        x_copy(i).wait()
        for j in range(WIDTH // 128):
            lanes = pl.ds(pl.multiple_of(i * WIDTH + j * 128, 128), 128)
            ext[j] = x_ref[:, lanes].astype(F4)
            base = 1 - w_ref.shape[0]
            tops = range(BLOCK, rows, BLOCK)
            for top, out in conv_rows(ext, j, w_ref[:, lanes], bias_ref[:, lanes], tops, base):
                out_ref[top : top + BLOCK, lanes] = out
            out_ref[0:BLOCK, lanes] = jnp.zeros((BLOCK, 128), BF)

    proj_copy.wait()


def conv_body(conv_in, conv_weight, conv_bias, proj_weight_t):
    arrays = (conv_in, conv_weight, conv_bias, proj_weight_t)
    rows, channels = conv_in.shape
    moved = 2 * sum(a.size * a.dtype.itemsize for a in arrays)
    return pl.pallas_call(
        conv_body_kernel,
        in_specs=[pl.BlockSpec(memory_space=pltpu.HBM)] * 4,
        out_specs=in_vmem(5),
        out_shape=[pltpu.VMEM(a.shape, a.dtype) for a in arrays]
        + [pltpu.VMEM((rows, channels), BF)],
        scratch_shapes=[
            pltpu.VMEM((WIDTH // 128, rows, 128), F4),
            pltpu.SemaphoreType.DMA((3,)),
            pltpu.SemaphoreType.DMA((channels // WIDTH,)),
        ],
        compiler_params=params(),
        cost_estimate=pl.CostEstimate(
            flops=20 * rows * channels, bytes_accessed=moved, transcendentals=rows * channels
        ),
        name="conv_body",
    )(*[in_hbm(a) for a in arrays])


def conv_kernel(
    x_ref, odd_ref, even_ref, w_ref, bias_ref, proj_ref, conv_ref, out_ref, part_ref, ext
):
    rows, channels = out_ref.shape
    rim = odd_ref.shape[0]
    base = rim - (w_ref.shape[0] - 1)
    odd = (lax.axis_index("seq") & 1) != 0

    @pl.loop(0, channels // WIDTH)
    def _(i):
        for j in range(WIDTH // 128):
            lanes = pl.ds(pl.multiple_of(i * WIDTH + j * 128, 128), 128)
            ext[j, 0:rim, :] = jnp.where(
                odd, odd_ref[:, lanes].astype(F4), even_ref[:, lanes].astype(F4)
            )
            ext[j, rim:, :] = x_ref[0:BLOCK, lanes].astype(F4)
            for top, out in conv_rows(ext, j, w_ref[:, lanes], bias_ref[:, lanes], (0,), base):
                out_ref[0:BLOCK, lanes] = out

    part_ref[...] = lax.dot_general(
        out_ref[...], proj_ref[...], NT, preferred_element_type=F4
    )


def conv_project(x, rims, w, bias, proj_weight_t, conv_out):
    rows, channels = conv_out.shape
    wide = proj_weight_t.shape[0]
    rim = rims[0].shape[0]
    return pl.pallas_call(
        conv_kernel,
        in_specs=in_vmem(7),
        out_specs=in_vmem(2),
        out_shape=[
            jax.ShapeDtypeStruct((rows, channels), BF),
            jax.ShapeDtypeStruct((rows, wide), F4),
        ],
        scratch_shapes=[pltpu.VMEM((WIDTH // 128, BLOCK + rim, 128), F4)],
        input_output_aliases={6: 0},
        compiler_params=params(),
        name="conv_project",
    )(x, *rims, w, bias, proj_weight_t, conv_out)


def in_hbm(a):
    return pltpu.with_memory_space_constraint(a, pltpu.HBM)


def in_vmem(count):
    return [pl.BlockSpec(memory_space=pltpu.VMEM)] * count


def split_sum(total, rank, out_ref):
    wide = total.shape[1]
    high = total.astype(BF)
    out_ref[:, :wide] = high
    out_ref[:, wide:] = (total[:, rank:] - high[:, rank:].astype(F4)).astype(BF)


def joined(ref, wide, rank):
    high = ref[:, :wide].astype(F4)
    return high[:, :rank], high[:, rank:] + ref[:, wide:].astype(F4)


def add_first(part, other, rank):
    rows, wide = part.shape

    def body(a_ref, b_ref, out_ref):
        split_sum(a_ref[...] + b_ref[...], rank, out_ref)

    return pl.pallas_call(
        body,
        in_specs=in_vmem(2),
        out_specs=pl.BlockSpec(memory_space=pltpu.VMEM),
        out_shape=jax.ShapeDtypeStruct((rows, 2 * wide - rank), BF),
        compiler_params=params(),
        name="add_first",
    )(part, other)


def add_later(mine, other, wide, rank):
    def body(a_ref, b_ref, out_ref):
        a_low, a_high = joined(a_ref, wide, rank)
        b_low, b_high = joined(b_ref, wide, rank)
        total = jnp.concatenate([a_low + b_low, a_high + b_high], axis=1)
        split_sum(total, rank, out_ref)

    return pl.pallas_call(
        body,
        in_specs=in_vmem(2),
        out_specs=pl.BlockSpec(memory_space=pltpu.VMEM),
        out_shape=jax.ShapeDtypeStruct(mine.shape, BF),
        compiler_params=params(),
        name="add_later",
    )(mine, other)


def softplus(x):
    u = jnp.exp(-jnp.abs(x))
    small = u * (1.0 - u * (0.5 - u * (1.0 / 3.0)))
    return jnp.maximum(x, 0.0) + jnp.where(u < 0.0078125, small, jnp.log(1.0 + u))


def wide_iota(shape, axis):
    return lax.broadcasted_iota(jnp.int32, shape, axis)


def contract(block, c_now, grad_now):
    mixed = jnp.dot(c_now, block, preferred_element_type=F4)
    pairs = lax.dot_general(grad_now, block, NT, preferred_element_type=F4)
    return mixed, pairs


def prepare_kernel(mine_ref, other_ref, proj_ref, b_ref, c_ref, alt_ref):
    rows, rank = proj_ref.shape
    wide = c_ref.shape[1]
    states = wide // BLOCK
    a_low, a_high = joined(mine_ref, rank + 2 * states, rank)
    b_low, b_high = joined(other_ref, rank + 2 * states, rank)
    proj_ref[...] = (a_low + b_low).astype(BF)
    ends = (a_high + b_high).astype(BF)
    lane = wide_iota((states, wide), 1)
    row = wide_iota((states, wide), 0)
    by_token = (lane % states == row).astype(BF)
    by_state = (lane // BLOCK == row).astype(BF)
    lane = wide_iota((rows, wide), 1)
    row = wide_iota((rows, wide), 0) % BLOCK
    c_mat = ends[:, states:]
    tiled = jnp.dot(c_mat, by_token, preferred_element_type=F4)
    c_ref[...] = jnp.where(lane // states == row, tiled, 0.0).astype(BF)
    tiled = jnp.dot(c_mat, by_state, preferred_element_type=F4)
    alt_ref[...] = jnp.where(lane % BLOCK == row, tiled, 0.0).astype(BF)
    tiled = jnp.dot(ends[:, :states], by_token, preferred_element_type=F4)
    b_diag = jnp.where(lane // states == row, tiled, 0.0).astype(BF)
    ones = jnp.ones((BLOCK, 128), BF)
    for top in range(0, rows, BLOCK):
        b_ref[top * states : (top + BLOCK) * states, :] = lax.dot_general(
            b_diag[top : top + BLOCK, :], ones, TN, preferred_element_type=F4
        )


def prepare(mine, other, rank, states):
    rows = mine.shape[0]
    wide = BLOCK * states
    return pl.pallas_call(
        prepare_kernel,
        in_specs=in_vmem(2),
        out_specs=in_vmem(4),
        out_shape=[
            jax.ShapeDtypeStruct((rows, rank), BF),
            jax.ShapeDtypeStruct((rows * states, 128), F4),
            jax.ShapeDtypeStruct((rows, wide), BF),
            jax.ShapeDtypeStruct((rows, wide), BF),
        ],
        compiler_params=params(),
        name="prepare",
    )(mine, other)


def pack_sums(total_ref, send_ref, folded):
    states, per = folded.shape
    width = states * per
    for n in range(states):
        folded[n : n + 1, :] = total_ref[:, n * per : (n + 1) * per]
    high = folded[...].astype(BF)
    send_ref[:, width : width + per] = high
    send_ref[:, width + per :] = (folded[...] - high.astype(F4)).astype(BF)


def unpack_sums(got_ref, sum_ref, folded):
    states, per = folded.shape
    width = states * per
    folded[...] = got_ref[:, width : width + per].astype(F4) + got_ref[:, width + per :].astype(F4)
    for n in range(states):
        sum_ref[:, n * per : (n + 1) * per] = folded[n : n + 1, :]


def message_width(width, states):
    return width + 2 * (width // states)


def scan_kernel(
    base, fresh,
    proj_ref, b_ref, c_ref, dtw_ref, dtb_ref, rate_ref, skip_ref, conv_ref, grad_ref, pairs_in,
    mixed_ref, cum_ref, end_ref, send_ref, total_ref, pairs_ref,
    raw, step, drive, folded, even, odd,
):
    rows = conv_ref.shape[0]
    states = rate_ref.shape[0]
    chunks = mixed_ref.shape[1] // WIDTH
    pairs_ref[...] = jnp.zeros_like(pairs_ref) if fresh else pairs_in[...]
    tri = (wide_iota((rows, rows), 0) >= wide_iota((rows, rows), 1)).astype(BF)

    def project(i):
        raw[...] = jnp.dot(proj_ref[...], dtw_ref[:, chunk_at(i, base)], preferred_element_type=F4)

    project(0)

    @pl.loop(0, chunks)
    def _(i):
        here = chunk_at(i)
        at_in = chunk_at(i, base)
        bias = dtb_ref[:, at_in]
        skip = skip_ref[:, at_in]
        rounded = []
        for top in range(0, rows, BLOCK):
            at = slice(top, top + BLOCK)
            now = softplus(raw[at, :] + bias)
            step[at, :] = now
            conv = conv_ref[at, at_in].astype(F4)
            drive[at, :] = now * conv
            mixed_ref[at, here] = skip * conv
            rounded.append(now.astype(BF))
        cum_ref[:, here] = jnp.dot(
            tri, jnp.concatenate(rounded, axis=0), preferred_element_type=F4
        )
        total_ref[:, here] = cum_ref[rows - 1 : rows, here]
        project(jnp.minimum(i + 1, chunks - 1))

        rate = rate_ref[:, at_in]
        state = jnp.zeros((states, WIDTH), F4)
        for top in range(0, rows, BLOCK):
            hist = odd if (top // BLOCK) % 2 else even
            for t in range(BLOCK):
                r = top + t
                b_now = b_ref[r * states : (r + 1) * states, :]
                b_now = jnp.concatenate([b_now] * (WIDTH // 128), axis=1)
                state = (
                    jnp.exp2(step[r : r + 1, :] * rate) * state + drive[r : r + 1, :] * b_now
                )
                hist[t * states : (t + 1) * states, :] = state.astype(BF)
            at = slice(top, top + BLOCK)
            mixed, pairs = contract(hist[...], c_ref[at, :], grad_ref[at, at_in])
            mixed_ref[at, here] += mixed
            pairs_ref[at, :] += pairs
        end_ref[:, here] = state
        send_ref[:, here] = state.astype(BF)

    pack_sums(total_ref, send_ref, folded)


def local_scan(base, width, prepared, dt_weight, dt_bias, rate, skip, conv_out, grad_out, pairs):
    rows = conv_out.shape[0]
    states = rate.shape[0]
    wide = BLOCK * states
    fresh = pairs is None
    proj, b_wide, c_wide, _ = prepared

    def body(*refs):
        refs = list(refs)
        if fresh:
            refs.insert(9, None)
        scan_kernel(base, fresh, *refs)

    ops = [proj, b_wide, c_wide, dt_weight, dt_bias, rate, skip, conv_out, grad_out]
    ops += [] if fresh else [pairs]
    work = rows * width * states
    return pl.pallas_call(
        body,
        in_specs=in_vmem(len(ops)),
        out_specs=in_vmem(6),
        out_shape=[
            jax.ShapeDtypeStruct((rows, width), F4),
            jax.ShapeDtypeStruct((rows, width), F4),
            jax.ShapeDtypeStruct((states, width), F4),
            jax.ShapeDtypeStruct((states, message_width(width, states)), BF),
            jax.ShapeDtypeStruct((1, width), F4),
            jax.ShapeDtypeStruct((rows, wide), F4),
        ],
        scratch_shapes=[
            pltpu.VMEM((rows, WIDTH), F4),
            pltpu.VMEM((rows, WIDTH), F4),
            pltpu.VMEM((rows, WIDTH), F4),
            pltpu.VMEM((states, width // states), F4),
            pltpu.VMEM((wide, WIDTH), BF),
            pltpu.VMEM((wide, WIDTH), BF),
        ],
        compiler_params=params(),
        cost_estimate=pl.CostEstimate(
            flops=600 * work, bytes_accessed=work, transcendentals=work
        ),
        name="local_scan",
    )(*ops)


def carry_kernel(
    base, scale, final,
    alt_ref, rate_ref, state_ref, cum_ref, mixed_ref, grad_ref, before_ref, local_ref, prev_ref,
    out_ref, result_ref,
    sums, rates, inits, even, odd,
):
    rows = cum_ref.shape[0]
    states = rate_ref.shape[0]
    wide = BLOCK * states
    i = pl.program_id(0)

    @pl.when(i == 0)
    def _():
        sums[...] = jnp.zeros_like(sums)

    here = chunk_at(i)
    at_in = chunk_at(i, base)
    for n in range(states):
        at = slice(n * BLOCK, (n + 1) * BLOCK)
        shape = (BLOCK, WIDTH)
        rates[at, :] = jnp.broadcast_to(rate_ref[n : n + 1, at_in], shape).astype(BF)
        inits[at, :] = jnp.broadcast_to(state_ref[n : n + 1, here], shape).astype(BF)
    for top in range(0, rows, BLOCK):
        hist = odd if (top // BLOCK) % 2 else even
        tokens = slice(top, top + BLOCK)
        cum = cum_ref[tokens, here].astype(BF)
        grad = grad_ref[tokens, at_in]
        for n in range(states):
            at = slice(n * BLOCK, (n + 1) * BLOCK)
            now = jnp.exp2(cum * rates[at, :]) * inits[at, :]
            hist[at, :] = now
            pairs = now * grad
            parts = [pairs[:, k : k + 128] for k in range(0, WIDTH, 128)]
            low = (parts[0] + parts[1]).astype(F4)
            sums[n, tokens, :] += low + (parts[2] + parts[3]).astype(F4)
        mixed = jnp.dot(alt_ref[tokens, :], hist[...], preferred_element_type=F4)
        out_ref[tokens, :] = (mixed_ref[tokens, here] + mixed).astype(BF)

    @pl.when(i == pl.num_programs(0) - 1)
    def _():
        ones = jnp.ones((8, 256), BF)
        if final:
            lane = wide_iota((rows, wide), 1)
            row = wide_iota((rows, wide), 0) % BLOCK
            by_token = jnp.where(lane // states == row, local_ref[...], 0.0)
            pick = wide_iota((states, wide), 1) % states == wide_iota((states, wide), 0)
            result_ref[...] = before_ref[...] + lax.dot_general(
                pick.astype(F4), by_token, NT,
                preferred_element_type=F4, precision=lax.Precision.HIGHEST,
            )
        else:
            result_ref[...] = jnp.zeros_like(result_ref)
        for n in range(states):
            high = sums[n].astype(BF)
            low = (sums[n] - high.astype(F4)).astype(BF)
            both = jnp.concatenate([high, low], axis=1)
            line = lax.dot_general(ones, both, NT, preferred_element_type=F4)
            result_ref[n : n + 1, :] += line[0:1, :]
        if final:
            result_ref[...] = result_ref[...] * scale


def add_carry(base, scale, alt, rate, incoming, cum, mixed, grad_out, before, local, prev):
    rows, width = cum.shape
    states, channels = rate.shape
    wide = BLOCK * states
    final = local is not None
    ops = [alt, rate, incoming, cum, mixed, grad_out]
    specs = in_vmem(6)
    if final:
        ops += [before, local, prev]
        specs += in_vmem(2) + [pl.BlockSpec(memory_space=pl.ANY)]

    def body(*refs):
        refs = list(refs)
        if not final:
            refs[6:6] = [None] * 3
        carry_kernel(base, scale, final, *refs)

    work = rows * width * states
    return pl.pallas_call(
        body,
        grid=(width // WIDTH,),
        in_specs=specs,
        out_specs=[
            pl.BlockSpec((rows, WIDTH), lambda i: (0, i + base)),
            whole(states, rows),
        ],
        out_shape=[
            jax.ShapeDtypeStruct((rows, channels), BF),
            jax.ShapeDtypeStruct((states, rows), F4),
        ],
        scratch_shapes=[
            pltpu.VMEM((states, rows, 128), F4),
            pltpu.VMEM((wide, WIDTH), BF),
            pltpu.VMEM((wide, WIDTH), BF),
            pltpu.VMEM((wide, WIDTH), BF),
            pltpu.VMEM((wide, WIDTH), BF),
        ],
        input_output_aliases={len(ops) - 1: 0} if final else {},
        compiler_params=params(),
        cost_estimate=pl.CostEstimate(
            flops=300 * work, bytes_accessed=work, transcendentals=work
        ),
        name="add_carry",
    )(*ops)


def merge_kernel(
    base, bit, last, rate_ref, end_ref, total_ref, got_ref, pre_ref, psum_ref, *refs
):
    *outs, osum_ref, folded = refs
    later = (lax.axis_index("seq") & bit) != 0
    unpack_sums(got_ref, osum_ref, folded)
    for i in range(end_ref.shape[1] // WIDTH):
        at = slice(i * WIDTH, (i + 1) * WIDTH)
        rate = rate_ref[:, (base + i) * WIDTH : (base + i + 1) * WIDTH]
        fade = lambda s: jnp.exp2(rate * s)
        other = got_ref[:, at].astype(F4)
        prefix, before = pre_ref[:, at], psum_ref[:, at]
        outs[0][:, at] = jnp.where(later, prefix + fade(before) * other, prefix)
        if not last:
            total, osum, end = total_ref[:, at], osum_ref[:, at], end_ref[:, at]
            outs[1][:, at] = jnp.where(later, before + osum, before)
            first = jnp.where(later, other, end)
            second = jnp.where(later, end, other)
            end = second + fade(jnp.where(later, total, osum)) * first
            outs[2][:, at] = end
            outs[3][:, at] = end.astype(BF)
            outs[4][:, at] = total + osum
    if not last:
        pack_sums(outs[4], outs[3], folded)


def merge(base, bit, last, rate, end, total, got, prefix, prefix_sum):
    states, width = end.shape
    outs = [jax.ShapeDtypeStruct((states, width), F4)]
    if not last:
        outs += [
            jax.ShapeDtypeStruct((1, width), F4),
            jax.ShapeDtypeStruct((states, width), F4),
            jax.ShapeDtypeStruct(got.shape, BF),
            jax.ShapeDtypeStruct((1, width), F4),
        ]

    def body(*refs):
        merge_kernel(base, bit, last, *refs)

    return pl.pallas_call(
        body,
        in_specs=in_vmem(6),
        out_specs=in_vmem(len(outs)),
        out_shape=outs,
        scratch_shapes=[
            pltpu.VMEM((1, width), F4),
            pltpu.VMEM((states, width // states), F4),
        ],
        compiler_params=params(),
        name="merge",
    )(rate, end, total, got, prefix, prefix_sum)


def weight_first(parts, conv_out, count):
    states, rows = parts[0].shape
    share = conv_out.shape[1] // count
    many = len(parts)

    def body(*refs):
        conv_ref, out_ref = refs[many:]
        grad_c = refs[0][...]
        for r in refs[1:many]:
            grad_c = grad_c + r[...]
        high = grad_c.astype(BF)
        low = (grad_c - high.astype(F4)).astype(BF)
        both = jnp.concatenate([high, low], axis=0)
        for j in range(count):
            block = conv_ref[:, j * share : (j + 1) * share]
            out = jnp.dot(both, block, preferred_element_type=F4)
            out_ref[j] = (out[:states, :] + out[states:, :]).astype(BF)

    return pl.pallas_call(
        body,
        in_specs=in_vmem(many + 1),
        out_specs=pl.BlockSpec(memory_space=pltpu.VMEM),
        out_shape=jax.ShapeDtypeStruct((count, states, share), BF),
        compiler_params=params(),
        name="weight_first",
    )(*parts, conv_out)


def weight_gradient(parts, conv_out):
    count = lax.axis_size("seq")
    states = parts[0].shape[0]
    share = conv_out.shape[1] // count
    if share % 128 == 0:
        weight = weight_first(parts, conv_out, count)
    else:
        grad_c = sum(parts[1:], parts[0]).astype(BF)
        weight = jnp.dot(grad_c, conv_out, preferred_element_type=F4).astype(BF)
        weight = weight.reshape(states, count, share).transpose(1, 0, 2)
    weight = lax.all_to_all(weight, "seq", 0, 0)
    return jnp.sum(weight.astype(F4), axis=0).T


def exchange(base, bit, rate, held):
    end, send, total, prefix, prefix_sum = held
    last = 2 * bit >= lax.axis_size("seq")
    got = swap(send, "seq", bit)
    outs = merge(base, bit, last, rate, end, total, got, prefix, prefix_sum)
    if last:
        return outs[0]
    prefix, prefix_sum, end, send, total = outs
    return end, send, total, prefix, prefix_sum


def on_device(
    conv_in,
    conv_weight,
    conv_bias,
    proj_weight,
    dt_weight,
    dt_bias,
    decay_rate,
    skip_gain,
    grad_out,
):
    rows, channels = conv_in.shape
    taps = conv_weight.shape[0]
    rank = dt_weight.shape[0]
    states = decay_rate.shape[0]
    count = lax.axis_size("seq")
    tp = lax.axis_size("tp")
    rim_rows = 8 * -(-(taps - 1) // 8)
    edge = conv_in[rows - rim_rows :]
    rims = [
        lax.ppermute(edge, "seq", [p for i in range(k, count - 1, 2) for p in ((i, i + 1), (i + 1, i))])
        for k in range(2)
    ]
    x, w, bias, weight_t, conv_out = conv_body(
        conv_in, conv_weight, conv_bias[None], proj_weight.T
    )
    rate = decay_rate * (-LOG2E)
    conv_out, part = conv_project(x, rims, w, bias, weight_t, conv_out)
    mine = add_first(part, swap(part, "tp", 1), rank)
    other = swap(mine, "tp", 2)
    bit = 4
    while bit < tp:
        mine = add_later(mine, other, part.shape[1], rank)
        other = swap(mine, "tp", bit)
        bit *= 2
    prepared = prepare(mine, other, rank, states)

    width = channels // 2
    bases = (0, width // WIDTH)
    pairs = None
    local, held = [], []
    for base in bases:
        mixed, cum, end, send, total, pairs = local_scan(
            base, width, prepared, dt_weight, dt_bias[None], rate, skip_gain[None],
            conv_out, grad_out, pairs,
        )
        local.append((cum, mixed))
        held.append((end, send, total, jnp.zeros_like(end), jnp.zeros_like(total)))
    bit = 1
    while bit < count:
        held = [exchange(base, bit, rate, h) for base, h in zip(bases, held)]
        bit *= 2

    scale = 1.0 / (rows * count)
    shared = (scale, prepared[3], rate)
    mixed, more = add_carry(bases[0], *shared, held[0], *local[0], grad_out, None, None, None)
    mixed, grad_c = add_carry(bases[1], *shared, held[1], *local[1], grad_out, more, pairs, mixed)
    parts = [grad_c] + [swap(grad_c, "tp", k) for k in range(1, tp)]
    weight_grad = weight_gradient(parts, conv_out)
    return (mixed, weight_grad[None])


def solution(mesh):
    return jax.shard_map(
        on_device,
        mesh=mesh,
        in_specs=(
            P("seq", "tp"),
            P(None, "tp"),
            P("tp"),
            P("tp", None),
            P(None, "tp"),
            P("tp"),
            P(None, "tp"),
            P("tp"),
            P("seq", "tp"),
        ),
        out_specs=(P("seq", "tp"), P("tp", "seq", None)),
        check_vma=False,
    )
```
